128 devices in a mesh: rep: 8 (over y, x_hi), fsdp: 16 (over x_lo, z, core).
Axes of the slice: x: 4 (x_hi: 2, x_lo: 2; x = x_hi * 2 + x_lo), y: 4, z: 4, core: 2. Of those that a mesh axis runs over, the one named last changes fastest.
Arguments:
- tokens: bfloat16 [65536, 8192], P(('rep', 'fsdp')), may hold values from -6 to 6
- cotangent: bfloat16 [65536, 1024], P(('rep', 'fsdp')), may hold values from -1.5 to 1.5
- row_count: int32 [128], P(('rep', 'fsdp')), may hold values from 16 to 512, as said below
- destination: int32 [65536], P(('rep', 'fsdp')), may hold values from 0 to 15, as said below
- step: int32 [1], replicated, may hold values from 1 to 2999
- weight: float32 [8, 8192, 1024], P('rep', 'fsdp'), may hold values from -0.0625 to 0.0625
- weight_m: float32 [8, 8192, 1024], P('rep', 'fsdp'), may hold values from -12 to 12
- weight_v: float32 [8, 8192, 1024], P('rep', 'fsdp'), may hold values from 0.01 to 10
- gain: float32 [8, 8192], P('rep', 'fsdp'), may hold values from 0.25 to 1.75
- gain_m: float32 [8, 8192], P('rep', 'fsdp'), may hold values from -12 to 12
- gain_v: float32 [8, 8192], P('rep', 'fsdp'), may hold values from 0.01 to 10
Outputs:
- keys: bfloat16 [65536, 1024], P(('rep', 'fsdp'))
- weight_out: float32 [8, 8192, 1024], P('rep', 'fsdp')
- weight_m_out: float32 [8, 8192, 1024], P('rep', 'fsdp')
- weight_v_out: float32 [8, 8192, 1024], P('rep', 'fsdp')
- gain_out: float32 [8, 8192], P('rep', 'fsdp')
- gain_m_out: float32 [8, 8192], P('rep', 'fsdp')
- gain_v_out: float32 [8, 8192], P('rep', 'fsdp')
The draws below stay inside these ranges and needn't reach their ends.
Inputs may be any that keep to these rules, and one draw needn't show every extreme that they name: `row_count`: A multiple of 16. In every group the counts sum to 4096, and some device's count is 512. `destination`: at the live slots of a device with count c, each rank of the group is named exactly c / 16 times, so every rank trains exactly 256 rows; entries at other slots are unused.
All inputs are finite; a program needn't handle non-finite values.
Results may differ from the reference program's by a relative error of at most 0.017.
Values may be sent and summed in bfloat16 or wider, within the bound.
No kernel may reach another device: no remote copies, remote signals or barrier semaphores. Data moves between devices by JAX's collectives and lax.ppermute only.
A program may use at most 192 MiB of HBM per device.

```python
import math
import jax
import jax.numpy as jnp
from jax import lax

D = 8192
TOK_DEV = 512
KW = 1024
ROWS = 256
TOKENS = 65536
N_REP = 8
N_FSDP = 16
DEVICES = 128


def balance_plan(key):
    groups = N_FSDP
    reps = DEVICES // N_FSDP
    slot = TOK_DEV // groups
    extra = ROWS - slot - (groups - 1)
    seats = (groups - 1) * (slot - 1)

    def one_source(source_key, live_count):
        shuffled = jax.random.permutation(source_key, TOK_DEV)
        position = jnp.arange(TOK_DEV, dtype=jnp.int32)
        live = position < live_count
        earlier = (shuffled[None, :] < shuffled[:, None]) & live[None, :]
        live_rank = jnp.sum(earlier.astype(jnp.int32), axis=1)
        return live_rank % groups

    def one_group(group_key):
        pick_key, bias_key, noise_key, order_key, dead_key = jax.random.split(group_key, 5)
        full_source = jax.random.randint(pick_key, (), 0, groups)
        bias = jax.random.randint(bias_key, (groups - 1, 1), 0, 4)
        noise = jax.random.randint(noise_key, (groups - 1, slot - 1), 0, 65536)
        seat_index = jnp.arange(seats, dtype=jnp.int32).reshape(groups - 1, slot - 1)
        score = ((bias * 65536 + noise) * seats + seat_index).reshape(-1)
        ranked = jnp.argsort(jnp.argsort(-score))
        chosen = (ranked < extra).astype(jnp.int32).reshape(groups - 1, slot - 1)
        others = 1 + jnp.sum(chosen, axis=1)
        source = jnp.arange(groups, dtype=jnp.int32)
        other_index = jnp.clip(source - (source > full_source).astype(jnp.int32), 0, groups - 2)
        per_rank = jnp.where(source == full_source, slot, others[other_index])
        counts = (per_rank * groups).astype(jnp.int32)
        source_keys = jax.random.split(order_key, groups)
        dest = jax.vmap(one_source)(source_keys, counts)
        filler = jax.random.randint(dead_key, (groups, TOK_DEV), 0, groups)
        live_all = jnp.arange(TOK_DEV, dtype=jnp.int32)[None, :] < counts[:, None]
        dest = jnp.where(live_all, dest, filler).astype(jnp.int32)
        return (counts, dest.reshape(-1))
    group_keys = jax.random.split(key, reps)
    counts, dests = jax.vmap(one_group)(group_keys)
    return (counts.reshape(-1), dests.reshape(-1))


def draw_row_count(key, part):
    counts, dests = balance_plan(jax.random.fold_in(key, 17))
    return counts


def draw_destination(key, part):
    counts, dests = balance_plan(jax.random.fold_in(key, 17))
    return dests


def block_scale(stream_key, extent, pieces, low, top_value):
    def one(dim, parts):
        heights = jax.random.uniform(jax.random.fold_in(jax.random.fold_in(stream_key, 6), dim), (parts,), jnp.float32, low / len(pieces), top_value / len(pieces))
        return jnp.repeat(jnp.exp(heights), extent[dim] // parts).reshape((-1,) + (1,) * (len(extent) - dim - 1))

    factor_of = one(*pieces[0])
    for cut in pieces[1:]:
        factor_of = factor_of * one(*cut)
    return factor_of


def normal_values(stream_key, extent, spread, reach, cuts=(), kind=jnp.bfloat16):
    array = spread * jax.random.normal(stream_key, extent, jnp.float32)
    if cuts:
        array = array * block_scale(stream_key, extent, cuts, -0.22, 0.18)
    return jnp.clip(array, -reach, reach).astype(kind)


def setup_inputs(seed: int = 0) -> dict:
    key_list = jax.random.split(jax.random.key(seed), 12)
    tokens = normal_values(key_list[0], (TOKENS, D), 1.0, 6.0, ((0, 128),))
    cotangent = normal_values(key_list[1], (TOKENS, KW), 0.25, 1.5, ((0, 128),))
    row_count = draw_row_count(jax.random.fold_in(key_list[11], 71), 0)
    destination = draw_destination(jax.random.fold_in(key_list[11], 71), 0)
    step = jax.random.randint(key_list[4], (1,), 1, 3000).astype(jnp.int32)
    weight = normal_values(key_list[5], (N_REP, D, KW), D ** -0.5, 0.0625, ((0, 8), (1, 16)), jnp.float32)
    weight_m = normal_values(key_list[6], (N_REP, D, KW), 2.0, 12.0, ((0, 8), (1, 16)), jnp.float32)
    weight_v = jnp.clip(jnp.exp(math.log(10.0) - 6.9077553 * jax.random.uniform(key_list[7], (N_REP, D, KW), jnp.float32) ** block_scale(key_list[7], (N_REP, D, KW), ((0, 8), (1, 16)), -0.2, 0.2)), 0.01, 10.0)
    gain = jnp.clip(1.0 + 0.15 * jax.random.normal(key_list[8], (N_REP, D), jnp.float32), 0.25, 1.75)
    gain_m = normal_values(key_list[9], (N_REP, D), 2.0, 12.0, ((0, 8), (1, 16)), jnp.float32)
    gain_v = jnp.clip(jnp.exp(math.log(10.0) - 6.9077553 * jax.random.uniform(key_list[10], (N_REP, D), jnp.float32) ** block_scale(key_list[10], (N_REP, D), ((0, 8), (1, 16)), -0.2, 0.2)), 0.01, 10.0)
    return {"tokens": tokens, "cotangent": cotangent, "row_count": row_count, "destination": destination, "step": step, "weight": weight, "weight_m": weight_m, "weight_v": weight_v, "gain": gain, "gain_m": gain_m, "gain_v": gain_v}


BETA_ONE = 0.9
BETA_TWO = 0.95
LEARN_RATE = 0.00015
WEIGHT_DECAY = 0.1
ADAM_EPS = 1e-08
NORM_EPS = 1e-05

def group_work(tokens, cotangent, row_count, destination, weight, gain):
    groups = N_FSDP
    slot = TOK_DEV // groups
    total_rows = groups * TOK_DEV
    flat = jnp.arange(total_rows, dtype=jnp.int32)
    source = flat // TOK_DEV
    live = flat % TOK_DEV < row_count[source]
    order_key = jnp.where(live, destination * total_rows + flat, groups * total_rows + flat)
    order = jnp.argsort(order_key)[:groups * ROWS].reshape(groups, ROWS).astype(jnp.int32)
    per_rank = row_count // groups
    starts = (jnp.cumsum(per_rank) - per_rank).astype(jnp.int32)
    narrow = weight.astype(jnp.bfloat16)
    narrow_gain = gain.astype(jnp.bfloat16).astype(jnp.float32)

    def rank_step(carry, picked):
        grad_w, grad_gain = carry
        rows = tokens[picked].astype(jnp.float32)
        rstd = lax.rsqrt(lax.optimization_barrier(jnp.mean(rows * rows, axis=1, keepdims=True)) + NORM_EPS)
        unit = rows * rstd
        normed = (unit * narrow_gain).astype(jnp.bfloat16)
        row_keys = jnp.dot(normed, narrow, preferred_element_type=jnp.float32).astype(jnp.bfloat16)
        upstream = cotangent[picked]
        part = jnp.dot(normed.T, upstream, preferred_element_type=jnp.float32)
        part = lax.optimization_barrier(part.astype(jnp.bfloat16)).astype(jnp.float32)
        back = jnp.dot(upstream, narrow.T, preferred_element_type=jnp.float32)
        return ((grad_w + part, grad_gain + lax.optimization_barrier(jnp.sum(back * unit, axis=0))), row_keys)
    init = (jnp.zeros((D, KW), jnp.float32), jnp.zeros((D,), jnp.float32))
    (grad_w, grad_gain), row_keys = lax.scan(rank_step, init, order)
    anchor = order // TOK_DEV
    slots = anchor * slot + jnp.arange(ROWS, dtype=jnp.int32)[None, :] - starts[anchor]
    rank_index = jnp.broadcast_to(jnp.arange(groups, dtype=jnp.int32)[:, None], (groups, ROWS))
    placed = jnp.zeros((groups, TOK_DEV, KW), jnp.bfloat16).at[rank_index, slots].set(row_keys)
    return (placed.reshape(total_rows, KW), grad_w, grad_gain)

def reference(tokens, cotangent, row_count, destination, step, weight, weight_m, weight_v, gain, gain_m, gain_v):
    reps = N_REP
    per_group = (tokens.reshape(reps, N_FSDP * TOK_DEV, D), cotangent.reshape(reps, N_FSDP * TOK_DEV, KW), row_count.reshape(reps, N_FSDP), destination.reshape(reps, N_FSDP * TOK_DEV), weight, gain)
    keys, grad_w, grad_gain = lax.map(lambda packed: group_work(*packed), per_group)
    t = step[0]
    count = (t + 1).astype(jnp.float32)
    fix_one = 1.0 - jnp.power(jnp.float32(BETA_ONE), count)
    fix_two = 1.0 - jnp.power(jnp.float32(BETA_TWO), count)

    def adam(param, first, second, grad, decay):
        first_new = BETA_ONE * first + (1.0 - BETA_ONE) * grad
        second_new = BETA_TWO * second + (1.0 - BETA_TWO) * grad * grad
        direction = first_new / fix_one / (jnp.sqrt(second_new / fix_two) + ADAM_EPS)
        return (param - LEARN_RATE * (direction + decay * param), first_new, second_new)
    w_new, m_new, v_new = adam(weight, weight_m, weight_v, grad_w, WEIGHT_DECAY)
    g_new, gm_new, gv_new = adam(gain, gain_m, gain_v, grad_gain, 0.0)
    bits = min(3, int(N_REP).bit_length() - 1)
    chosen_bit = t % bits
    partner = jnp.bitwise_xor(jnp.arange(reps, dtype=jnp.int32), jnp.left_shift(jnp.int32(1), chosen_bit))
    weight_out = 0.5 * (w_new + w_new[partner])
    gain_out = 0.5 * (g_new + g_new[partner])
    return (keys.reshape(reps * N_FSDP * TOK_DEV, KW), weight_out, m_new, v_new, gain_out, gm_new, gv_new)
```

```python
import jax
import jax.numpy as jnp
from jax import lax
from jax.sharding import PartitionSpec as P

BETA_ONE = 0.9
BETA_TWO = 0.95
LEARN_RATE = 0.00015
WEIGHT_DECAY = 0.1
ADAM_EPS = 1e-08
NORM_EPS = 1e-05


def as_sent(x):
    return jax.tree.map(lambda a: a.astype(jnp.bfloat16) if a.dtype == jnp.float32 else a, x)


def partner(x, axis, stride):
    return lax.ppermute(x, axis, [(i, i ^ 1 << stride) for i in range(lax.axis_size(axis))])


def adam(param, first, second, grad, decay, fix_one, fix_two):
    first_new = BETA_ONE * first + (1.0 - BETA_ONE) * grad
    second_new = BETA_TWO * second + (1.0 - BETA_TWO) * grad * grad
    direction = first_new / fix_one / (jnp.sqrt(second_new / fix_two) + ADAM_EPS)
    return (param - LEARN_RATE * (direction + decay * param), first_new, second_new)


def partner_of(bit):
    return lambda pair: jax.tree.map(
        lambda part, own: part.astype(own.dtype), partner(as_sent(pair), "rep", bit), pair
    )


def placement(row_count, destination, groups, slot):
    rows = destination.shape[0]
    position = jnp.arange(rows, dtype=jnp.int32)
    live = position < row_count[0]
    same = (destination[:, None] == destination[None, :]) & (position[None, :] < position[:, None])
    within = jnp.sum(same.astype(jnp.int32), axis=1)
    target = jnp.where(live, destination * slot + within, -1)
    return live, (position[:, None] == target[None, :]).astype(jnp.bfloat16)


def body(
    tokens,
    cotangent,
    row_count,
    destination,
    step,
    weight,
    weight_m,
    weight_v,
    gain,
    gain_m,
    gain_v,
):
    groups = lax.axis_size("fsdp")
    rows = tokens.shape[0]
    key_width = cotangent.shape[1]
    slot = rows // groups
    live, place = placement(row_count, destination, groups, slot)
    narrow = weight[0].astype(jnp.bfloat16).astype(jnp.float32)
    narrow_gain = gain[0].astype(jnp.bfloat16).astype(jnp.float32)
    scaled = (narrow * narrow_gain[:, None]).astype(jnp.bfloat16)
    full_scaled = lax.all_gather(scaled, "fsdp", axis=0, tiled=True)
    rows_float = tokens.astype(jnp.float32)
    rstd = lax.rsqrt(jnp.mean(rows_float * rows_float, axis=1, keepdims=True) + NORM_EPS)
    upstream = jnp.where(live[:, None], cotangent.astype(jnp.float32) * rstd, 0.0).astype(jnp.bfloat16)
    unit_grad = lax.psum_scatter(
        lax.dot_general(
            tokens, upstream, (((0,), (0,)), ((), ())), preferred_element_type=jnp.float32
        ).astype(jnp.bfloat16),
        "fsdp",
        scatter_dimension=0,
        tiled=True,
    ).astype(jnp.float32)
    row_keys = (
        jnp.dot(tokens, full_scaled, preferred_element_type=jnp.float32) * rstd
    ).astype(jnp.bfloat16)
    placed = jnp.dot(place, row_keys, preferred_element_type=jnp.float32).astype(jnp.bfloat16)
    keys = lax.all_to_all(
        placed.reshape(groups, slot, key_width), "fsdp", split_axis=0, concat_axis=0, tiled=True
    ).reshape(rows, key_width)
    weight_grad = unit_grad * narrow_gain[:, None]
    gain_grad = jnp.sum(unit_grad * narrow, axis=1)
    t = step[0]
    count = (t + 1).astype(jnp.float32)
    fix_one = 1.0 - jnp.power(jnp.float32(BETA_ONE), count)
    fix_two = 1.0 - jnp.power(jnp.float32(BETA_TWO), count)
    w_new, m_new, v_new = adam(
        weight[0], weight_m[0], weight_v[0], weight_grad, WEIGHT_DECAY, fix_one, fix_two
    )
    g_new, gm_new, gv_new = adam(gain[0], gain_m[0], gain_v[0], gain_grad, 0.0, fix_one, fix_two)
    bits = min(3, lax.axis_size("rep").bit_length() - 1)
    branches = [partner_of(bit) for bit in range(bits)]
    other_w, other_g = lax.switch(t % bits, branches, (w_new, g_new))
    weight_out = 0.5 * (w_new + other_w)
    gain_out = 0.5 * (g_new + other_g)
    return (
        keys,
        weight_out[None],
        m_new[None],
        v_new[None],
        gain_out[None],
        gm_new[None],
        gv_new[None],
    )


def solution(mesh):
    return jax.shard_map(
        body,
        mesh=mesh,
        in_specs=(
            P(("rep", "fsdp"), None),
            P(("rep", "fsdp"), None),
            P(("rep", "fsdp")),
            P(("rep", "fsdp")),
            P(),
            P("rep", "fsdp", None),
            P("rep", "fsdp", None),
            P("rep", "fsdp", None),
            P("rep", "fsdp"),
            P("rep", "fsdp"),
            P("rep", "fsdp"),
        ),
        out_specs=(
            P(("rep", "fsdp"), None),
            P("rep", "fsdp", None),
            P("rep", "fsdp", None),
            P("rep", "fsdp", None),
            P("rep", "fsdp"),
            P("rep", "fsdp"),
            P("rep", "fsdp"),
        ),
        check_vma=False,
    )
```

```python
import functools

import jax
import jax.numpy as jnp
from jax import lax
from jax.experimental import pallas as pl
from jax.experimental.pallas import tpu as pltpu
from jax.sharding import PartitionSpec as P


BETA_ONE = 0.9
BETA_TWO = 0.95
LEARN_RATE = 0.00015
WEIGHT_DECAY = 0.1
ADAM_EPS = 1e-08
NORM_EPS = 1e-05


BF16, F32, I32 = jnp.bfloat16, jnp.float32, jnp.int32
NX, NZ, NC = 2, 4, 2
PLACES = (
    *((0, 2), (1, 2), (1, 1), (0, 3), (0, 0), (1, 0), (0, 1), (1, 3)),
    *((0, 0), (0, 3), (0, 1), (0, 2), (1, 0), (1, 3), (1, 1), (1, 2)),
)
SEND_PAD = 16


def shape(dims, dtype):
    return jax.ShapeDtypeStruct(dims, dtype)


def place_id(x, z, c):
    return (x % NX * NZ + z % NZ) * NC + c % NC


def shift(a, dx, dz, dc):
    pairs = [
        (place_id(x, z, c), place_id(x + dx, z + dz, c + dc))
        for x in range(NX)
        for z in range(NZ)
        for c in range(NC)
    ]
    return lax.ppermute(a, "fsdp", pairs)


def cost(flops, moved):
    return pl.CostEstimate(flops=flops, transcendentals=0, bytes_accessed=moved)


def prep_kernel(info, own_ref, x_ref, cot_ref, other_ref, up_ref, rstd_ref, acc_ref, *, width):
    j = pl.program_id(0)
    rows, block = x_ref.shape
    other_ref[...] = x_ref[...]
    tile = 64
    for r in range(0, rows, tile):
        parts = [jnp.zeros((tile, 128), F32)] * 4
        for q in range(0, block, 128):
            for k, ref in enumerate((own_ref, x_ref)):
                v = ref[r : r + tile, q : q + 128].astype(F32)
                k += 2 * (q // 128 % 2)
                parts[k] = parts[k] + v * v
        part = (parts[0] + parts[1]) + (parts[2] + parts[3])
        acc_ref[r : r + tile, :] = jnp.where(j == 0, part, acc_ref[r : r + tile, :] + part)

    @pl.when(j == pl.num_programs(0) - 1)
    def _():
        count = info[1]
        for r in range(0, rows, tile):
            total = jnp.sum(acc_ref[r : r + tile, :], axis=1, keepdims=True)
            rstd = lax.rsqrt(total * (1.0 / width) + NORM_EPS)
            rstd_ref[r : r + tile, :] = jnp.broadcast_to(rstd, (tile, 128))
            row = lax.broadcasted_iota(I32, (tile, 1), 0) + r
            scale = jnp.where(row < count, rstd, 0.0)
            up_ref[r : r + tile, :] = (cot_ref[r : r + tile, :].astype(F32) * scale).astype(BF16)


def prep(info, tokens, cotangent):
    rows, width = tokens.shape
    key_width = cotangent.shape[1]
    block = width // (NX * NZ * NC)
    whole = lambda j, s: (0, 0)
    return pl.pallas_call(
        functools.partial(prep_kernel, width=width),
        grid_spec=pltpu.PrefetchScalarGridSpec(
            num_scalar_prefetch=1,
            grid=(NX * NZ,),
            in_specs=[
                pl.BlockSpec((rows, block), lambda j, s: (0, 2 * j + s[0])),
                pl.BlockSpec((rows, block), lambda j, s: (0, 2 * j + 1 - s[0])),
                pl.BlockSpec((rows, key_width), whole),
            ],
            out_specs=[
                pl.BlockSpec((rows, block), lambda j, s: (0, j)),
                pl.BlockSpec((rows, key_width), whole),
                pl.BlockSpec((rows, 128), whole),
            ],
            scratch_shapes=[pltpu.VMEM((rows, 128), F32)],
        ),
        out_shape=[
            shape((rows, width // 2), BF16),
            shape((rows, key_width), BF16),
            shape((rows, 128), F32),
        ],
        cost_estimate=cost(3 * rows * width, 3 * rows * width),
        name="prep",
    )(info, tokens, tokens, cotangent)


def over_rows(a, b):
    return lax.dot_general(a, b, (((0,), (0,)), ((), ())), preferred_element_type=F32)


def grad_kernel(table, xa_ref, xb_ref, ua_ref, ub_ref, *refs, n_add, splits):
    adds, outs = refs[:n_add], refs[n_add:]
    s = pl.program_id(0)
    width = xa_ref.shape[1]
    first = 0
    for k, per in enumerate(splits):

        @pl.when(s == k)
        def _(first=first, per=per, k=k):
            tile = width // per
            for p in range(per):
                cols = slice(p * tile, (p + 1) * tile)
                total = over_rows(xa_ref[:, cols], ua_ref[...]) + over_rows(
                    xb_ref[:, cols], ub_ref[...]
                )
                if n_add:
                    total = total + adds[k][cols, :].astype(F32)
                out = outs[first + p]
                out[...] = total.astype(out.dtype)

        first += per


def grad_blocks(table, at, tokens, other, up_own, up_other, adds, dtype, splits, cut=1, part=0):
    rows, width = tokens.shape
    block = width // (NX * NZ * NC) // cut
    key_width = up_own.shape[1]
    n = len(splits)
    whole = lambda s, t: (0, 0)
    outs = [shape((block // per, key_width), dtype) for per in splits for _ in range(per)]
    return pl.pallas_call(
        functools.partial(grad_kernel, n_add=len(adds), splits=splits),
        grid_spec=pltpu.PrefetchScalarGridSpec(
            num_scalar_prefetch=1,
            grid=(n,),
            in_specs=[
                pl.BlockSpec((rows, block), lambda s, t: (0, t[at + s] * cut + part)),
                pl.BlockSpec((rows, block), lambda s, t: (0, t[len(PLACES) + at + s] * cut + part)),
                pl.BlockSpec((rows, key_width), whole),
                pl.BlockSpec((rows, key_width), whole),
            ]
            + [pl.BlockSpec((block, key_width), lambda s, t: (part, 0)) for _ in adds],
            out_specs=[pl.BlockSpec(o.shape, whole) for o in outs],
        ),
        out_shape=outs,
        cost_estimate=cost(
            4 * n * rows * block * key_width,
            4 * n * rows * block + 4 * rows * key_width + 2 * n * block * key_width,
        ),
    )(table, tokens, other, up_own, up_other, *adds)


def add_kernel(own, near, far, out):
    total = own[...] + near[...].astype(F32) + far[...].astype(F32)
    out[...] = total.astype(BF16)


def add_half(h, own, near, far):
    half, cols = far.shape
    whole_map = lambda i: (2 * h + i, 0)
    return pl.pallas_call(
        add_kernel,
        grid=(2,),
        in_specs=[
            pl.BlockSpec((half // 2, cols), whole_map),
            pl.BlockSpec((half // 2, cols), whole_map),
            pl.BlockSpec((half // 2, cols), lambda i: (i, 0)),
        ],
        out_specs=pl.BlockSpec((half // 2, cols), lambda i: (i, 0)),
        out_shape=shape((half, cols), BF16),
        cost_estimate=cost(2 * half * cols, 10 * half * cols),
    )(own, near, far)


def keys_kernel(table, *refs, n, n_acc):
    xa, xb, rest = refs[:n], refs[n : 2 * n], refs[2 * n :]
    w, rest = rest[: 2 * n], rest[2 * n :]
    accs, outs = rest[:n_acc], rest[n_acc:]
    for x_refs, k in ((xa, 0), (xb, 1)):
        total = accs[k][...] if n_acc else None
        for i, w_ref in enumerate(w):
            depth = w_ref.shape[0]
            lhs = x_refs[i // 2][:, i % 2 * depth : (i % 2 + 1) * depth]
            term = jnp.dot(lhs, w_ref[...], preferred_element_type=F32)
            total = term if total is None else total + term
        outs[k][...] = total.astype(outs[k].dtype)


def keys_part(table, at, tokens, other, pieces, accs, out_dtypes):
    rows, width = tokens.shape
    block = width // (NX * NZ * NC)
    key_width = pieces[0].shape[1]
    tile = rows // 2
    n = len(pieces) // 2
    view_a = lambda q: pl.BlockSpec((tile, block), lambda r, t: (r, t[at + q]))
    view_b = lambda q: pl.BlockSpec((tile, block), lambda r, t: (r, t[len(PLACES) + at + q]))
    out_spec = pl.BlockSpec((tile, key_width), lambda r, t: (r, 0))
    return pl.pallas_call(
        functools.partial(keys_kernel, n=n, n_acc=len(accs)),
        grid_spec=pltpu.PrefetchScalarGridSpec(
            num_scalar_prefetch=1,
            grid=(rows // tile,),
            in_specs=[view_a(q) for q in range(n)]
            + [view_b(q) for q in range(n)]
            + [pl.BlockSpec(w.shape, lambda r, t: (0, 0)) for w in pieces]
            + [out_spec for _ in accs],
            out_specs=[out_spec, out_spec],
        ),
        out_shape=[shape((rows, key_width), d) for d in out_dtypes],
        cost_estimate=cost(
            4 * n * rows * block * key_width,
            4 * n * rows * block + 2 * n * block * key_width + 8 * rows * key_width,
        ),
    )(table, *([tokens] * n), *([other] * n), *pieces, *accs)


def adam_step(param, first, second, grad, decay, fix_one, fix_two):
    first_new = BETA_ONE * first + (1.0 - BETA_ONE) * grad
    second_new = BETA_TWO * second + (1.0 - BETA_TWO) * grad * grad
    direction = first_new / fix_one / (jnp.sqrt(second_new / fix_two) + ADAM_EPS)
    return (param - LEARN_RATE * (direction + decay * param), first_new, second_new)


def adam_kernel(fix, own, near, far, got, w, m, v, g_row, gm, gv, g_col, *refs):
    (w_new, m_new, v_new, g_new, gm_new, gv_new, sent, fold_ref) = refs[-8:]
    i = pl.program_id(0)
    rows, cols = own.shape
    fix_one, fix_two = fix[0], fix[1]
    tile = 32

    @pl.when(i < pl.num_programs(0) - 1)
    def _():
        for r in range(0, rows, tile):
            sl = slice(r, r + tile)
            unit = own[sl, :] + near[sl, :].astype(F32) + far[sl, :].astype(F32)
            unit = unit + got[sl, :].astype(F32)
            weight = w[sl, :]
            narrow = weight.astype(BF16).astype(F32)
            gain = g_col[sl, :1].astype(BF16).astype(F32)
            new, first, second = adam_step(
                weight, m[sl, :], v[sl, :], unit * gain, WEIGHT_DECAY, fix_one, fix_two
            )
            w_new[sl, :], m_new[sl, :], v_new[sl, :] = new, first, second
            sent[sl, :] = new.astype(BF16)
            prod = unit * narrow
            fold = prod[:, :128]
            for q in range(128, cols, 128):
                fold = fold + prod[:, q : q + 128]
            at = pl.ds(pl.multiple_of(i * rows + r, tile), tile)
            fold_ref[at, :] = fold

    @pl.when(i == pl.num_programs(0) - 1)
    def _():
        grad = lax.dot_general(
            jnp.ones((8, 128), F32),
            fold_ref[...],
            (((1,), (1,)), ((), ())),
            precision=lax.Precision.HIGHEST,
            preferred_element_type=F32,
        )[:1, :]
        new, first, second = adam_step(g_row[...], gm[...], gv[...], grad, 0.0, fix_one, fix_two)
        g_new[...], gm_new[...], gv_new[...] = new, first, second
        wide = jnp.broadcast_to(new, (SEND_PAD, new.shape[1])).astype(BF16)
        sent[:SEND_PAD, : new.shape[1]] = wide
        sent[:SEND_PAD, new.shape[1] :] = jnp.zeros((SEND_PAD, cols - new.shape[1]), BF16)


ROW_TILES = 4


def adam_half(h, fix, own, near, far, got, w, m, v, g, gm, gv, g_col, carried):
    rows, cols = w.shape
    half = rows // 2
    tile = half // ROW_TILES
    last = ROW_TILES - 1
    whole = lambda i, *_: (0, 0)
    mat = pl.BlockSpec((tile, cols), lambda i, *_: (h * ROW_TILES + jnp.minimum(i, last), 0))
    new_mat = pl.BlockSpec((tile, cols), lambda i, *_: (jnp.minimum(i, last), 0))
    vec = pl.BlockSpec((1, half), lambda i, *_: (0, h))
    inputs = [own, near, far, got, w, m, v, g, gm, gv, g_col]
    specs = [mat, new_mat, mat, new_mat, mat, mat, mat, vec, vec, vec]
    col_map = lambda i, *_: (h * ROW_TILES + jnp.minimum(i, last), 0)
    specs += [pl.BlockSpec((tile, g_col.shape[1]), col_map)]
    n_in = 1 + len(inputs)
    return pl.pallas_call(
        adam_kernel,
        grid_spec=pltpu.PrefetchScalarGridSpec(
            num_scalar_prefetch=1,
            grid=(ROW_TILES + 1,),
            in_specs=specs + [pl.BlockSpec(memory_space=pl.ANY)] * len(carried),
            out_specs=[new_mat, mat, mat, pl.BlockSpec((1, half), whole), vec, vec]
            + [pl.BlockSpec((tile, cols), lambda i, *_: (i, 0))],
            scratch_shapes=[pltpu.VMEM((half, 128), F32)],
        ),
        out_shape=[
            shape((half, cols), F32),
            shape((rows, cols), F32),
            shape((rows, cols), F32),
            shape((1, half), F32),
            shape((1, rows), F32),
            shape((1, rows), F32),
            shape((half + SEND_PAD, cols), BF16),
        ],
        input_output_aliases={n_in + k: o for k, o in zip(range(len(carried)), (1, 2, 4, 5))},
        cost_estimate=cost(20 * half * cols, 30 * half * cols),
    )(fix, *inputs, *carried)


def mean_kernel(w, g, got, got_gain, *refs):
    w_out, g_out = refs[-2:]
    w_out[...] = 0.5 * (w[...] + got[...].astype(F32))
    g_out[...] = 0.5 * (g[...] + got_gain[:, : g.shape[1]].astype(F32)[:1, :])


def mean_half(h, w_new, g_new, got, carried):
    half, cols = w_new.shape
    rows = 2 * half
    tile = half // ROW_TILES
    whole = lambda i: (0, 0)
    row = lambda i: (i, 0)
    return pl.pallas_call(
        mean_kernel,
        grid=(ROW_TILES,),
        in_specs=[
            pl.BlockSpec((tile, cols), row),
            pl.BlockSpec(g_new.shape, whole),
            pl.BlockSpec((tile, cols), row),
            pl.BlockSpec((SEND_PAD, cols), lambda i: (half // SEND_PAD, 0)),
        ]
        + [pl.BlockSpec(memory_space=pl.ANY)] * len(carried),
        out_specs=[
            pl.BlockSpec((tile, cols), lambda i: (h * ROW_TILES + i, 0)),
            pl.BlockSpec((1, half), lambda i: (0, h)),
        ],
        out_shape=[shape((rows, cols), F32), shape((1, rows), F32)],
        input_output_aliases={4 + k: k for k in range(len(carried))},
        cost_estimate=cost(2 * half * cols, 10 * half * cols),
    )(w_new, g_new, got, got, *carried)


def finish(bit, reduced, fix, state, g_col, key_parts):
    give, keep, two_up, two_down, three_up, three_down, got = reduced
    part_own, more, rstd, place = key_parts
    groups = lax.axis_size("fsdp")
    rows, key_width = part_own.shape

    def send(message):
        pairs = [(i, i ^ 1 << bit) for i in range(lax.axis_size("rep"))]
        return lax.ppermute(message, "rep", pairs)

    last = shift(add_half(1, give, two_up, three_down[1]), 1, 0, 0)
    row_keys = ((part_own + more.astype(F32)) * rstd[:, :1]).astype(BF16)
    placed = jnp.dot(place, row_keys, preferred_element_type=F32).astype(BF16)
    keys = lax.all_to_all(
        placed.reshape(groups, rows // groups, key_width),
        "fsdp",
        split_axis=0,
        concat_axis=0,
        tiled=True,
    ).reshape(rows, key_width)
    updated, heard, carried = [], [], ()
    for h, other in ((0, got), (1, last)):
        w_new, m, v, g_new, gm, gv, sent = adam_half(
            h, fix, keep, three_up[h], two_down, other, *state, g_col, carried
        )
        carried = (m, v, gm, gv)
        updated.append((w_new, g_new))
        heard.append(send(sent))
    outs = ()
    for h in range(2):
        outs = mean_half(h, *updated[h], heard[h], outs)
    return keys, *outs, *carried


def placement(count, destination, slot):
    rows = destination.shape[0]
    position = jnp.arange(rows, dtype=I32)
    live = position < count
    same = (destination[:, None] == destination[None, :]) & (position[None, :] < position[:, None])
    within = jnp.sum(same.astype(I32), axis=1)
    target = jnp.where(live, destination * slot + within, -1)
    return (position[:, None] == target[None, :]).astype(BF16)


def body(
    tokens,
    cotangent,
    row_count,
    destination,
    step,
    weight,
    weight_m,
    weight_v,
    gain,
    gain_m,
    gain_v,
):
    groups = lax.axis_size("fsdp")
    rows = tokens.shape[0]
    slot = rows // groups
    me = lax.axis_index("fsdp")
    c, z, x = me & 1, me >> 1 & 3, me >> 3
    info = jnp.stack([c, row_count[0]]).astype(I32)
    far_x, far_z = (jnp.array(v, I32) for v in zip(*PLACES))
    ids = ((x + far_x) & 1) * NZ + ((z + far_z) & 3)
    table = jnp.concatenate([2 * ids + c, ids])

    half = weight.shape[1] // 2
    tops = []
    for h in range(2):
        sl = slice(h * half, (h + 1) * half)
        narrow = weight[0, sl].astype(BF16).astype(F32)
        narrow_gain = gain[0, sl].astype(BF16).astype(F32)
        tops.append((narrow * narrow_gain[:, None]).astype(BF16))
    top, bottom = tops
    before_top = shift(top, 0, 1, 0)
    after_bottom = shift(bottom, 0, -1, 0)
    own_top = shift(top, 1, 0, 0)
    before_bottom = shift(bottom, 0, 1, 0)
    after_top = shift(top, 0, -1, 0)
    own_bottom = shift(bottom, 1, 0, 0)

    other_cols, up_own, rstd = prep(info, tokens, cotangent)
    other = shift(other_cols, 0, 0, 1)
    up_other = shift(up_own, 0, 0, 1)

    far_top = shift(before_top, 0, 1, 0)
    far_bottom = shift(after_bottom, 0, -1, 0)
    x_before = [shift(before_top, 1, 0, 0), shift(before_bottom, 1, 0, 0)]
    x_after = [shift(after_top, 1, 0, 0), shift(after_bottom, 1, 0, 0)]
    x_far = [shift(far_top, 1, 0, 0), shift(far_bottom, 1, 0, 0)]

    work = (tokens, other, up_own, up_other)
    first_up, first_down = grad_blocks(table, 0, *work, (), BF16, (1, 1))
    adds = (shift(first_up, 0, 1, 0), shift(first_down, 0, -1, 0))
    second_up, second_down = grad_blocks(table, 2, *work, (), BF16, (1, 1))
    two_up = shift(second_up, 0, 1, 0)
    two_down = shift(second_down, 0, -1, 0)
    keep, give = grad_blocks(table, 4, *work, (), F32, (1, 1))
    three_up, three_down = [], []
    for h in range(2):
        third = grad_blocks(table, 6, *work, adds, BF16, (1, 1), 2, h)
        three_up.append(shift(third[0], 0, 1, 0))
        three_down.append(shift(third[1], 0, -1, 0))
    got = shift(add_half(0, give, two_up, three_down[0]), 1, 0, 0)

    near = (top, bottom, before_top, before_bottom, after_top, after_bottom)
    accs = keys_part(table, 8, tokens, other, near, (), (F32, F32))
    near = (far_top, far_bottom, own_top, own_bottom, *x_before, *x_after)
    accs = keys_part(table, 11, tokens, other, near, accs, (F32, F32))
    part_own, part_other = keys_part(table, 15, tokens, other, x_far, accs, (F32, BF16))
    place = placement(row_count[0], destination, slot)
    more = shift(part_other, 0, 0, 1)

    t = step[0]
    count = (t + 1).astype(F32)
    fix = jnp.stack(
        [
            1.0 - jnp.power(jnp.float32(BETA_ONE), count),
            1.0 - jnp.power(jnp.float32(BETA_TWO), count),
        ]
    )
    bits = min(3, lax.axis_size("rep").bit_length() - 1)
    g_col = jnp.broadcast_to(gain[0][:, None], (gain.shape[1], 128))
    state = (weight[0], weight_m[0], weight_v[0], gain, gain_m, gain_v)
    keys, weight_out, gain_out, m_new, v_new, gm_new, gv_new = lax.switch(
        t % bits,
        [functools.partial(finish, b) for b in range(bits)],
        (give, keep, two_up, two_down, tuple(three_up), tuple(three_down), got),
        fix,
        state,
        g_col,
        (part_own, more, rstd, place),
    )
    return keys, weight_out[None], m_new[None], v_new[None], gain_out, gm_new, gv_new


def solution(mesh):
    both, group = P(("rep", "fsdp"), None), P(("rep", "fsdp"))
    mat, vec = P("rep", "fsdp", None), P("rep", "fsdp")
    return jax.shard_map(
        body,
        mesh=mesh,
        in_specs=(both, both, group, group, P(), mat, mat, mat, vec, vec, vec),
        out_specs=(both, mat, mat, mat, vec, vec, vec),
        check_vma=False,
    )
```

```python
import functools

import jax
import jax.numpy as jnp
from jax import lax
from jax.experimental import pallas as pl
from jax.experimental.pallas import tpu as pltpu
from jax.sharding import PartitionSpec as P


BETA_ONE = 0.9
BETA_TWO = 0.95
LEARN_RATE = 0.00015
WEIGHT_DECAY = 0.1
ADAM_EPS = 1e-08
NORM_EPS = 1e-05


BF16, F32, I32 = jnp.bfloat16, jnp.float32, jnp.int32
NX, NZ, NC = 2, 4, 2
PLACES = (
    *((0, 2), (1, 2), (1, 1), (0, 3), (0, 0), (1, 0), (0, 1), (1, 3)),
    *((0, 0), (0, 3), (0, 1), (0, 2), (1, 0), (1, 3), (1, 1), (1, 2)),
)
SEND_PAD = 16


def shape(dims, dtype):
    return jax.ShapeDtypeStruct(dims, dtype)


def place_id(x, z, c):
    return (x % NX * NZ + z % NZ) * NC + c % NC


def shift(a, dx, dz, dc):
    pairs = [
        (place_id(x, z, c), place_id(x + dx, z + dz, c + dc))
        for x in range(NX)
        for z in range(NZ)
        for c in range(NC)
    ]
    return lax.ppermute(a, "fsdp", pairs)


def cost(flops, moved):
    return pl.CostEstimate(flops=flops, transcendentals=0, bytes_accessed=moved)


def prep_kernel(info, own_ref, x_ref, cot_ref, other_ref, up_ref, rstd_ref, acc_ref, *, width):
    j = pl.program_id(0)
    rows, block = x_ref.shape
    other_ref[...] = x_ref[...]
    tile = 64
    for r in range(0, rows, tile):
        parts = [jnp.zeros((tile, 128), F32)] * 4
        for q in range(0, block, 128):
            for k, ref in enumerate((own_ref, x_ref)):
                v = ref[r : r + tile, q : q + 128].astype(F32)
                k += 2 * (q // 128 % 2)
                parts[k] = parts[k] + v * v
        part = (parts[0] + parts[1]) + (parts[2] + parts[3])
        acc_ref[r : r + tile, :] = jnp.where(j == 0, part, acc_ref[r : r + tile, :] + part)

    @pl.when(j == pl.num_programs(0) - 1)
    def _():
        count = info[1]
        for r in range(0, rows, tile):
            total = jnp.sum(acc_ref[r : r + tile, :], axis=1, keepdims=True)
            rstd = lax.rsqrt(total * (1.0 / width) + NORM_EPS)
            rstd_ref[r : r + tile, :] = jnp.broadcast_to(rstd, (tile, 128))
            row = lax.broadcasted_iota(I32, (tile, 1), 0) + r
            scale = jnp.where(row < count, rstd, 0.0)
            up_ref[r : r + tile, :] = (cot_ref[r : r + tile, :].astype(F32) * scale).astype(BF16)


def prep(info, tokens, cotangent):
    rows, width = tokens.shape
    key_width = cotangent.shape[1]
    block = width // (NX * NZ * NC)
    whole = lambda j, s: (0, 0)
    return pl.pallas_call(
        functools.partial(prep_kernel, width=width),
        grid_spec=pltpu.PrefetchScalarGridSpec(
            num_scalar_prefetch=1,
            grid=(NX * NZ,),
            in_specs=[
                pl.BlockSpec((rows, block), lambda j, s: (0, 2 * j + s[0])),
                pl.BlockSpec((rows, block), lambda j, s: (0, 2 * j + 1 - s[0])),
                pl.BlockSpec((rows, key_width), whole),
            ],
            out_specs=[
                pl.BlockSpec((rows, block), lambda j, s: (0, j)),
                pl.BlockSpec((rows, key_width), whole),
                pl.BlockSpec((rows, 128), whole),
            ],
            scratch_shapes=[pltpu.VMEM((rows, 128), F32)],
        ),
        out_shape=[
            shape((rows, width // 2), BF16),
            shape((rows, key_width), BF16),
            shape((rows, 128), F32),
        ],
        cost_estimate=cost(3 * rows * width, 3 * rows * width),
        name="prep",
    )(info, tokens, tokens, cotangent)


def over_rows(a, b):
    return lax.dot_general(a, b, (((0,), (0,)), ((), ())), preferred_element_type=F32)


def grad_kernel(table, xa_ref, xb_ref, ua_ref, ub_ref, *refs, n_add, splits):
    adds, outs = refs[:n_add], refs[n_add:]
    s = pl.program_id(0)
    width = xa_ref.shape[1]
    first = 0
    for k, per in enumerate(splits):

        @pl.when(s == k)
        def _(first=first, per=per, k=k):
            tile = width // per
            for p in range(per):
                cols = slice(p * tile, (p + 1) * tile)
                total = over_rows(xa_ref[:, cols], ua_ref[...]) + over_rows(
                    xb_ref[:, cols], ub_ref[...]
                )
                if n_add:
                    total = total + adds[k][cols, :].astype(F32)
                out = outs[first + p]
                out[...] = total.astype(out.dtype)

        first += per


def grad_blocks(table, at, tokens, other, up_own, up_other, adds, dtype, splits, cut=1, part=0):
    rows, width = tokens.shape
    block = width // (NX * NZ * NC) // cut
    key_width = up_own.shape[1]
    n = len(splits)
    whole = lambda s, t: (0, 0)
    outs = [shape((block // per, key_width), dtype) for per in splits for _ in range(per)]
    return pl.pallas_call(
        functools.partial(grad_kernel, n_add=len(adds), splits=splits),
        grid_spec=pltpu.PrefetchScalarGridSpec(
            num_scalar_prefetch=1,
            grid=(n,),
            in_specs=[
                pl.BlockSpec((rows, block), lambda s, t: (0, t[at + s] * cut + part)),
                pl.BlockSpec((rows, block), lambda s, t: (0, t[len(PLACES) + at + s] * cut + part)),
                pl.BlockSpec((rows, key_width), whole),
                pl.BlockSpec((rows, key_width), whole),
            ]
            + [pl.BlockSpec((block, key_width), lambda s, t: (part, 0)) for _ in adds],
            out_specs=[pl.BlockSpec(o.shape, whole) for o in outs],
        ),
        out_shape=outs,
        cost_estimate=cost(
            4 * n * rows * block * key_width,
            4 * n * rows * block + 4 * rows * key_width + 2 * n * block * key_width,
        ),
    )(table, tokens, other, up_own, up_other, *adds)


def add_kernel(own, near, far, out):
    tile = 64

    def step(r, _):
        sl = pl.ds(pl.multiple_of(r * tile, tile), tile)
        total = own[sl, :] + near[sl, :].astype(F32) + far[sl, :].astype(F32)
        out[sl, :] = total.astype(BF16)
        return 0

    lax.fori_loop(0, own.shape[0] // tile, step, 0)


def add_half(h, own, near, far):
    half, cols = far.shape
    part = pl.BlockSpec((half, cols), lambda i: (h, 0))
    whole = pl.BlockSpec((half, cols), lambda i: (0, 0))
    return pl.pallas_call(
        add_kernel,
        grid=(1,),
        in_specs=[part, part, whole],
        out_specs=whole,
        out_shape=shape((half, cols), BF16),
        cost_estimate=cost(2 * half * cols, 10 * half * cols),
    )(own, near, far)


def keys_kernel(table, *refs, n, n_acc):
    xa, xb, rest = refs[:n], refs[n : 2 * n], refs[2 * n :]
    w, rest = rest[: 2 * n], rest[2 * n :]
    accs, outs = rest[:n_acc], rest[n_acc:]
    for x_refs, k in ((xa, 0), (xb, 1)):
        total = accs[k][...] if n_acc else None
        for i, w_ref in enumerate(w):
            depth = w_ref.shape[0]
            lhs = x_refs[i // 2][:, i % 2 * depth : (i % 2 + 1) * depth]
            term = jnp.dot(lhs, w_ref[...], preferred_element_type=F32)
            total = term if total is None else total + term
        outs[k][...] = total.astype(outs[k].dtype)


def keys_part(table, at, tokens, other, pieces, accs, out_dtypes):
    rows, width = tokens.shape
    block = width // (NX * NZ * NC)
    key_width = pieces[0].shape[1]
    tile = rows // 2
    n = len(pieces) // 2
    view_a = lambda q: pl.BlockSpec((tile, block), lambda r, t: (r, t[at + q]))
    view_b = lambda q: pl.BlockSpec((tile, block), lambda r, t: (r, t[len(PLACES) + at + q]))
    out_spec = pl.BlockSpec((tile, key_width), lambda r, t: (r, 0))
    return pl.pallas_call(
        functools.partial(keys_kernel, n=n, n_acc=len(accs)),
        grid_spec=pltpu.PrefetchScalarGridSpec(
            num_scalar_prefetch=1,
            grid=(rows // tile,),
            in_specs=[view_a(q) for q in range(n)]
            + [view_b(q) for q in range(n)]
            + [pl.BlockSpec(w.shape, lambda r, t: (0, 0)) for w in pieces]
            + [out_spec for _ in accs],
            out_specs=[out_spec, out_spec],
        ),
        out_shape=[shape((rows, key_width), d) for d in out_dtypes],
        cost_estimate=cost(
            4 * n * rows * block * key_width,
            4 * n * rows * block + 2 * n * block * key_width + 8 * rows * key_width,
        ),
    )(table, *([tokens] * n), *([other] * n), *pieces, *accs)


def adam_step(param, first, second, grad, decay, fix_one, fix_two):
    first_new = BETA_ONE * first + (1.0 - BETA_ONE) * grad
    second_new = BETA_TWO * second + (1.0 - BETA_TWO) * grad * grad
    direction = first_new / fix_one / (jnp.sqrt(second_new / fix_two) + ADAM_EPS)
    return (param - LEARN_RATE * (direction + decay * param), first_new, second_new)


def adam_kernel(fix, own, near, far, got, w, m, v, g_row, gm, gv, g_col, *refs):
    (w_new, m_new, v_new, g_new, gm_new, gv_new, sent, fold_ref) = refs[-8:]
    rows, cols = own.shape
    fix_one, fix_two = fix[0], fix[1]
    tile = 32

    def step(r, _):
        sl = pl.ds(pl.multiple_of(r * tile, tile), tile)
        unit = own[sl, :] + near[sl, :].astype(F32) + far[sl, :].astype(F32)
        unit = unit + got[sl, :].astype(F32)
        weight = w[sl, :]
        narrow = weight.astype(BF16).astype(F32)
        gain = g_col[sl, :1].astype(BF16).astype(F32)
        new, first, second = adam_step(
            weight, m[sl, :], v[sl, :], unit * gain, WEIGHT_DECAY, fix_one, fix_two
        )
        w_new[sl, :], m_new[sl, :], v_new[sl, :] = new, first, second
        sent[sl, :] = new.astype(BF16)
        prod = unit * narrow
        fold = prod[:, :128]
        for q in range(128, cols, 128):
            fold = fold + prod[:, q : q + 128]
        fold_ref[sl, :] = fold
        return 0

    lax.fori_loop(0, rows // tile, step, 0)
    grad = lax.dot_general(
        jnp.ones((8, 128), F32),
        fold_ref[...],
        (((1,), (1,)), ((), ())),
        precision=lax.Precision.HIGHEST,
        preferred_element_type=F32,
    )[:1, :]
    new, first, second = adam_step(g_row[...], gm[...], gv[...], grad, 0.0, fix_one, fix_two)
    g_new[...], gm_new[...], gv_new[...] = new, first, second
    sent[rows:, :] = jnp.zeros((sent.shape[0] - rows, cols), BF16)
    sent[rows:, :rows] = jnp.broadcast_to(new, (sent.shape[0] - rows, rows)).astype(BF16)


def adam_half(h, fix, own, near, far, got, w, m, v, g, gm, gv, g_col, carried):
    rows, cols = w.shape
    half = rows // 2
    whole = lambda i, *_: (0, 0)
    row_half = lambda i, *_: (h, 0)
    mat = pl.BlockSpec((half, cols), row_half)
    new_mat = pl.BlockSpec((half, cols), whole)
    vec = pl.BlockSpec((1, half), lambda i, *_: (0, h))
    inputs = [own, near, far, got, w, m, v, g, gm, gv, g_col]
    specs = [mat, new_mat, mat, new_mat, mat, mat, mat, vec, vec, vec]
    specs += [pl.BlockSpec((half, g_col.shape[1]), row_half)]
    n_in = 1 + len(inputs)
    return pl.pallas_call(
        adam_kernel,
        grid_spec=pltpu.PrefetchScalarGridSpec(
            num_scalar_prefetch=1,
            grid=(1,),
            in_specs=specs + [pl.BlockSpec(memory_space=pl.ANY)] * len(carried),
            out_specs=[new_mat, mat, mat, pl.BlockSpec((1, half), whole), vec, vec]
            + [pl.BlockSpec((half + SEND_PAD, cols), whole)],
            scratch_shapes=[pltpu.VMEM((half, 128), F32)],
        ),
        out_shape=[
            shape((half, cols), F32),
            shape((rows, cols), F32),
            shape((rows, cols), F32),
            shape((1, half), F32),
            shape((1, rows), F32),
            shape((1, rows), F32),
            shape((half + SEND_PAD, cols), BF16),
        ],
        input_output_aliases={n_in + k: o for k, o in zip(range(len(carried)), (1, 2, 4, 5))},
        cost_estimate=cost(20 * half * cols, 30 * half * cols),
    )(fix, *inputs, *carried)


def mean_kernel(w, g, got, *refs):
    w_out, g_out = refs[-2:]
    rows = w.shape[0]
    tile = 64

    def step(r, _):
        sl = pl.ds(pl.multiple_of(r * tile, tile), tile)
        w_out[sl, :] = 0.5 * (w[sl, :] + got[sl, :].astype(F32))
        return 0

    lax.fori_loop(0, rows // tile, step, 0)
    g_out[...] = 0.5 * (g[...] + got[rows:, :rows].astype(F32)[:1, :])


def mean_half(h, w_new, g_new, got, carried):
    half, cols = w_new.shape
    rows = 2 * half
    whole = lambda i: (0, 0)
    return pl.pallas_call(
        mean_kernel,
        grid=(1,),
        in_specs=[pl.BlockSpec(a.shape, whole) for a in (w_new, g_new, got)]
        + [pl.BlockSpec(memory_space=pl.ANY)] * len(carried),
        out_specs=[
            pl.BlockSpec((half, cols), lambda i: (h, 0)),
            pl.BlockSpec((1, half), lambda i: (0, h)),
        ],
        out_shape=[shape((rows, cols), F32), shape((1, rows), F32)],
        input_output_aliases={3 + k: k for k in range(len(carried))},
        cost_estimate=cost(2 * half * cols, 10 * half * cols),
    )(w_new, g_new, got, *carried)


def placed_kernel(own, more, rstd, place, out):
    row_keys = ((own[...] + more[...].astype(F32)) * rstd[:, :1]).astype(BF16)
    out[...] = jnp.dot(place[...], row_keys, preferred_element_type=F32).astype(BF16)


def placed_keys(own, more, rstd, place):
    return pl.pallas_call(
        placed_kernel,
        out_shape=shape(own.shape, BF16),
        cost_estimate=cost(2 * place.size * own.shape[1], 8 * own.size),
        name="placed",
    )(own, more, rstd, place)


def copy_kernel(a, out):
    out[...] = a[...]


def store_keys(a):
    return pl.pallas_call(
        copy_kernel,
        out_shape=shape(a.shape, a.dtype),
        grid=(2,),
        in_specs=[pl.BlockSpec((a.shape[0] // 2, a.shape[1]), lambda i: (i, 0))],
        out_specs=pl.BlockSpec((a.shape[0] // 2, a.shape[1]), lambda i: (i, 0)),
        cost_estimate=cost(0, 4 * a.size),
        name="store",
    )(a)


def finish(bit, reduced, fix, state, g_col, placed):
    give, keep, two_up, two_down, three_up, three_down, got = reduced
    groups = lax.axis_size("fsdp")
    rows, key_width = placed.shape

    def send(message):
        pairs = [(i, i ^ 1 << bit) for i in range(lax.axis_size("rep"))]
        return lax.ppermute(message, "rep", pairs)

    last = shift(add_half(1, give, two_up, three_down[1]), 1, 0, 0)
    keys = lax.all_to_all(
        placed.reshape(groups, rows // groups, key_width),
        "fsdp",
        split_axis=0,
        concat_axis=0,
        tiled=True,
    ).reshape(rows, key_width)
    updated, heard, carried = [], [], ()
    for h, other in ((0, got), (1, last)):
        w_new, m, v, g_new, gm, gv, sent = adam_half(
            h, fix, keep, three_up[h], two_down, other, *state, g_col, carried
        )
        carried = (m, v, gm, gv)
        updated.append((w_new, g_new))
        heard.append(send(sent))
    outs = ()
    for h in range(2):
        outs = mean_half(h, *updated[h], heard[h], outs)
    return store_keys(keys), *outs, *carried


def placement(count, destination, slot):
    rows = destination.shape[0]
    position = jnp.arange(rows, dtype=I32)
    live = position < count
    same = (destination[:, None] == destination[None, :]) & (position[None, :] < position[:, None])
    within = jnp.sum(same.astype(I32), axis=1)
    target = jnp.where(live, destination * slot + within, -1)
    return (position[:, None] == target[None, :]).astype(BF16)


def body(
    tokens,
    cotangent,
    row_count,
    destination,
    step,
    weight,
    weight_m,
    weight_v,
    gain,
    gain_m,
    gain_v,
):
    groups = lax.axis_size("fsdp")
    rows = tokens.shape[0]
    slot = rows // groups
    me = lax.axis_index("fsdp")
    c, z, x = me & 1, me >> 1 & 3, me >> 3
    info = jnp.stack([c, row_count[0]]).astype(I32)
    far_x, far_z = (jnp.array(v, I32) for v in zip(*PLACES))
    ids = ((x + far_x) & 1) * NZ + ((z + far_z) & 3)
    table = jnp.concatenate([2 * ids + c, ids])

    half = weight.shape[1] // 2
    tops = []
    for h in range(2):
        sl = slice(h * half, (h + 1) * half)
        narrow = weight[0, sl].astype(BF16).astype(F32)
        narrow_gain = gain[0, sl].astype(BF16).astype(F32)
        tops.append((narrow * narrow_gain[:, None]).astype(BF16))
    top, bottom = tops
    before_top = shift(top, 0, 1, 0)
    after_bottom = shift(bottom, 0, -1, 0)
    own_top = shift(top, 1, 0, 0)
    before_bottom = shift(bottom, 0, 1, 0)
    after_top = shift(top, 0, -1, 0)
    own_bottom = shift(bottom, 1, 0, 0)

    other_cols, up_own, rstd = prep(info, tokens, cotangent)
    other = shift(other_cols, 0, 0, 1)
    up_other = shift(up_own, 0, 0, 1)

    far_top = shift(before_top, 0, 1, 0)
    far_bottom = shift(after_bottom, 0, -1, 0)
    x_before = [shift(before_top, 1, 0, 0), shift(before_bottom, 1, 0, 0)]
    x_after = [shift(after_top, 1, 0, 0), shift(after_bottom, 1, 0, 0)]
    x_far = [shift(far_top, 1, 0, 0), shift(far_bottom, 1, 0, 0)]

    work = (tokens, other, up_own, up_other)
    first_up, first_down = grad_blocks(table, 0, *work, (), BF16, (1, 1))
    adds = (shift(first_up, 0, 1, 0), shift(first_down, 0, -1, 0))
    second_up, second_down = grad_blocks(table, 2, *work, (), BF16, (1, 1))
    two_up = shift(second_up, 0, 1, 0)
    two_down = shift(second_down, 0, -1, 0)
    keep, give = grad_blocks(table, 4, *work, (), F32, (1, 1))
    three_up, three_down = [], []
    for h in range(2):
        third = grad_blocks(table, 6, *work, adds, BF16, (1, 1), 2, h)
        three_up.append(shift(third[0], 0, 1, 0))
        three_down.append(shift(third[1], 0, -1, 0))
    got = shift(add_half(0, give, two_up, three_down[0]), 1, 0, 0)

    near = (top, bottom, before_top, before_bottom, after_top, after_bottom)
    accs = keys_part(table, 8, tokens, other, near, (), (F32, F32))
    near = (far_top, far_bottom, own_top, own_bottom, *x_before, *x_after)
    accs = keys_part(table, 11, tokens, other, near, accs, (F32, F32))
    part_own, part_other = keys_part(table, 15, tokens, other, x_far, accs, (F32, BF16))
    place = placement(row_count[0], destination, slot)
    placed = placed_keys(part_own, shift(part_other, 0, 0, 1), rstd, place)

    t = step[0]
    count = (t + 1).astype(F32)
    fix = jnp.stack(
        [
            1.0 - jnp.power(jnp.float32(BETA_ONE), count),
            1.0 - jnp.power(jnp.float32(BETA_TWO), count),
        ]
    )
    bits = min(3, lax.axis_size("rep").bit_length() - 1)
    g_col = jnp.broadcast_to(gain[0][:, None], (gain.shape[1], 128))
    state = (weight[0], weight_m[0], weight_v[0], gain, gain_m, gain_v)
    keys, weight_out, gain_out, m_new, v_new, gm_new, gv_new = lax.switch(
        t % bits,
        [functools.partial(finish, b) for b in range(bits)],
        (give, keep, two_up, two_down, tuple(three_up), tuple(three_down), got),
        fix,
        state,
        g_col,
        placed,
    )
    return keys, weight_out[None], m_new[None], v_new[None], gain_out, gm_new, gv_new


def solution(mesh):
    both, group = P(("rep", "fsdp"), None), P(("rep", "fsdp"))
    mat, vec = P("rep", "fsdp", None), P("rep", "fsdp")
    return jax.shard_map(
        body,
        mesh=mesh,
        in_specs=(both, both, group, group, P(), mat, mat, mat, vec, vec, vec),
        out_specs=(both, mat, mat, mat, vec, vec, vec),
        check_vma=False,
    )
```

```python
import functools

import jax
import jax.numpy as jnp
from jax import lax
from jax.experimental import pallas as pl
from jax.experimental.pallas import tpu as pltpu
from jax.sharding import PartitionSpec as P


BETA_ONE = 0.9
BETA_TWO = 0.95
LEARN_RATE = 0.00015
WEIGHT_DECAY = 0.1
ADAM_EPS = 1e-08
NORM_EPS = 1e-05


BF16, F32, I32 = jnp.bfloat16, jnp.float32, jnp.int32
NX, NZ, NC = 2, 4, 2
PLACES = (
    *((0, 2), (1, 2), (1, 1), (0, 3), (0, 0), (1, 0), (0, 1), (1, 3)),
    *((0, 0), (0, 3), (0, 1), (0, 2), (1, 0), (1, 3), (1, 1), (1, 2)),
)
SEND_PAD = 16


def shape(dims, dtype):
    return jax.ShapeDtypeStruct(dims, dtype)


def place_id(x, z, c):
    return (x % NX * NZ + z % NZ) * NC + c % NC


def shift(a, dx, dz, dc):
    pairs = [
        (place_id(x, z, c), place_id(x + dx, z + dz, c + dc))
        for x in range(NX)
        for z in range(NZ)
        for c in range(NC)
    ]
    return lax.ppermute(a, "fsdp", pairs)


def cost(flops, moved):
    return pl.CostEstimate(flops=flops, transcendentals=0, bytes_accessed=moved)


def prep_kernel(info, x_ref, cot_ref, up_ref, rstd_ref, acc_ref, *, width):
    j = pl.program_id(0)
    rows, block = x_ref.shape
    tile = 64
    for r in range(0, rows, tile):
        parts = [jnp.zeros((tile, 128), F32)] * 4
        for q in range(0, block, 128):
            v = x_ref[r : r + tile, q : q + 128].astype(F32)
            k = q // 128 % 4
            parts[k] = parts[k] + v * v
        part = (parts[0] + parts[1]) + (parts[2] + parts[3])
        acc_ref[r : r + tile, :] = jnp.where(j == 0, part, acc_ref[r : r + tile, :] + part)

    @pl.when(j == pl.num_programs(0) - 1)
    def _():
        count = info[0]
        for r in range(0, rows, tile):
            total = jnp.sum(acc_ref[r : r + tile, :], axis=1, keepdims=True)
            rstd = lax.rsqrt(total * (1.0 / width) + NORM_EPS)
            rstd_ref[r : r + tile, :] = jnp.broadcast_to(rstd, (tile, 128))
            row = lax.broadcasted_iota(I32, (tile, 1), 0) + r
            scale = jnp.where(row < count, rstd, 0.0)
            up_ref[r : r + tile, :] = (cot_ref[r : r + tile, :].astype(F32) * scale).astype(BF16)


def prep(count, tokens, cotangent):
    rows, width = tokens.shape
    key_width = cotangent.shape[1]
    steps = 8
    whole = lambda j, s: (0, 0)
    return pl.pallas_call(
        functools.partial(prep_kernel, width=width),
        grid_spec=pltpu.PrefetchScalarGridSpec(
            num_scalar_prefetch=1,
            grid=(steps,),
            in_specs=[
                pl.BlockSpec((rows, width // steps), lambda j, s: (0, j)),
                pl.BlockSpec((rows, key_width), whole),
            ],
            out_specs=[pl.BlockSpec((rows, key_width), whole), pl.BlockSpec((rows, 128), whole)],
            scratch_shapes=[pltpu.VMEM((rows, 128), F32)],
        ),
        out_shape=[shape((rows, key_width), BF16), shape((rows, 128), F32)],
        cost_estimate=cost(3 * rows * width, 2 * rows * width),
        name="prep",
    )(count, tokens, cotangent)


def over_rows(a, b):
    return lax.dot_general(a, b, (((0,), (0,)), ((), ())), preferred_element_type=F32)


def grad_kernel(table, xa_ref, xb_ref, ua_ref, ub_ref, *refs, n_add, splits):
    adds, outs = refs[:n_add], refs[n_add:]
    s = pl.program_id(0)
    width = xa_ref.shape[1]
    first = 0
    for k, per in enumerate(splits):

        @pl.when(s == k)
        def _(first=first, per=per, k=k):
            tile = width // per
            for p in range(per):
                cols = slice(p * tile, (p + 1) * tile)
                total = over_rows(xa_ref[:, cols], ua_ref[...]) + over_rows(
                    xb_ref[:, cols], ub_ref[...]
                )
                if n_add:
                    total = total + adds[k][cols, :].astype(F32)
                out = outs[first + p]
                out[...] = total.astype(out.dtype)

        first += per


def grad_blocks(table, at, tokens, other, up_own, up_other, adds, dtype, splits, cut=1, part=0):
    rows, width = tokens.shape
    block = width // (NX * NZ * NC) // cut
    key_width = up_own.shape[1]
    n = len(splits)
    whole = lambda s, t: (0, 0)
    outs = [shape((block // per, key_width), dtype) for per in splits for _ in range(per)]
    return pl.pallas_call(
        functools.partial(grad_kernel, n_add=len(adds), splits=splits),
        grid_spec=pltpu.PrefetchScalarGridSpec(
            num_scalar_prefetch=1,
            grid=(n,),
            in_specs=[
                pl.BlockSpec((rows, block), lambda s, t: (0, t[at + s] * cut + part)),
                pl.BlockSpec((rows, block), lambda s, t: (0, t[at + s] * cut + part)),
                pl.BlockSpec((rows, key_width), whole),
                pl.BlockSpec((rows, key_width), whole),
            ]
            + [pl.BlockSpec((block, key_width), lambda s, t: (part, 0)) for _ in adds],
            out_specs=[pl.BlockSpec(o.shape, whole) for o in outs],
        ),
        out_shape=outs,
        cost_estimate=cost(
            4 * n * rows * block * key_width,
            4 * n * rows * block + 4 * rows * key_width + 2 * n * block * key_width,
        ),
    )(table, tokens, other, up_own, up_other, *adds)


def add_kernel(own, near, far, out):
    tile = 64

    def step(r, _):
        sl = pl.ds(pl.multiple_of(r * tile, tile), tile)
        total = own[sl, :] + near[sl, :].astype(F32) + far[sl, :].astype(F32)
        out[sl, :] = total.astype(BF16)
        return 0

    lax.fori_loop(0, own.shape[0] // tile, step, 0)


def add_half(h, own, near, far):
    half, cols = far.shape
    part = pl.BlockSpec((half, cols), lambda i: (h, 0))
    whole = pl.BlockSpec((half, cols), lambda i: (0, 0))
    return pl.pallas_call(
        add_kernel,
        grid=(1,),
        in_specs=[part, part, whole],
        out_specs=whole,
        out_shape=shape((half, cols), BF16),
        cost_estimate=cost(2 * half * cols, 10 * half * cols),
    )(own, near, far)


def keys_kernel(table, *refs, n, n_acc):
    xa, xb, rest = refs[:n], refs[n : 2 * n], refs[2 * n :]
    w, rest = rest[: 2 * n], rest[2 * n :]
    accs, outs = rest[:n_acc], rest[n_acc:]
    for x_refs, k in ((xa, 0), (xb, 1)):
        total = accs[k][...] if n_acc else None
        for i, w_ref in enumerate(w):
            depth = w_ref.shape[0]
            lhs = x_refs[i // 2][:, i % 2 * depth : (i % 2 + 1) * depth]
            term = jnp.dot(lhs, w_ref[...], preferred_element_type=F32)
            total = term if total is None else total + term
        outs[k][...] = total.astype(outs[k].dtype)


def keys_part(table, at, tokens, other, pieces, accs, out_dtypes):
    rows, width = tokens.shape
    block = width // (NX * NZ * NC)
    key_width = pieces[0].shape[1]
    tile = rows // 2
    n = len(pieces) // 2
    view_a = lambda q: pl.BlockSpec((tile, block), lambda r, t: (r, t[at + q]))
    view_b = lambda q: pl.BlockSpec((tile, block), lambda r, t: (r, t[at + q]))
    out_spec = pl.BlockSpec((tile, key_width), lambda r, t: (r, 0))
    return pl.pallas_call(
        functools.partial(keys_kernel, n=n, n_acc=len(accs)),
        grid_spec=pltpu.PrefetchScalarGridSpec(
            num_scalar_prefetch=1,
            grid=(rows // tile,),
            in_specs=[view_a(q) for q in range(n)]
            + [view_b(q) for q in range(n)]
            + [pl.BlockSpec(w.shape, lambda r, t: (0, 0)) for w in pieces]
            + [out_spec for _ in accs],
            out_specs=[out_spec, out_spec],
        ),
        out_shape=[shape((rows, key_width), d) for d in out_dtypes],
        cost_estimate=cost(
            4 * n * rows * block * key_width,
            4 * n * rows * block + 2 * n * block * key_width + 8 * rows * key_width,
        ),
    )(table, *([tokens] * n), *([other] * n), *pieces, *accs)


def adam_step(param, first, second, grad, decay, fix_one, fix_two):
    first_new = BETA_ONE * first + (1.0 - BETA_ONE) * grad
    second_new = BETA_TWO * second + (1.0 - BETA_TWO) * grad * grad
    direction = first_new / fix_one / (jnp.sqrt(second_new / fix_two) + ADAM_EPS)
    return (param - LEARN_RATE * (direction + decay * param), first_new, second_new)


def adam_kernel(fix, own, near, far, got, w, m, v, g_row, gm, gv, g_col, *refs):
    (w_new, m_new, v_new, g_new, gm_new, gv_new, sent, fold_ref) = refs[-8:]
    rows, cols = own.shape
    fix_one, fix_two = fix[0], fix[1]
    tile = 32

    def step(r, _):
        sl = pl.ds(pl.multiple_of(r * tile, tile), tile)
        unit = own[sl, :] + near[sl, :].astype(F32) + far[sl, :].astype(F32)
        unit = unit + got[sl, :].astype(F32)
        weight = w[sl, :]
        narrow = weight.astype(BF16).astype(F32)
        gain = g_col[sl, :1].astype(BF16).astype(F32)
        new, first, second = adam_step(
            weight, m[sl, :], v[sl, :], unit * gain, WEIGHT_DECAY, fix_one, fix_two
        )
        w_new[sl, :], m_new[sl, :], v_new[sl, :] = new, first, second
        sent[sl, :] = new.astype(BF16)
        prod = unit * narrow
        fold = prod[:, :128]
        for q in range(128, cols, 128):
            fold = fold + prod[:, q : q + 128]
        fold_ref[sl, :] = fold
        return 0

    lax.fori_loop(0, rows // tile, step, 0)
    grad = lax.dot_general(
        jnp.ones((8, 128), F32),
        fold_ref[...],
        (((1,), (1,)), ((), ())),
        precision=lax.Precision.HIGHEST,
        preferred_element_type=F32,
    )[:1, :]
    new, first, second = adam_step(g_row[...], gm[...], gv[...], grad, 0.0, fix_one, fix_two)
    g_new[...], gm_new[...], gv_new[...] = new, first, second
    sent[rows:, :] = jnp.zeros((sent.shape[0] - rows, cols), BF16)
    sent[rows:, :rows] = jnp.broadcast_to(new, (sent.shape[0] - rows, rows)).astype(BF16)


def adam_half(h, fix, own, near, far, got, w, m, v, g, gm, gv, g_col, carried):
    rows, cols = w.shape
    half = rows // 2
    whole = lambda i, *_: (0, 0)
    row_half = lambda i, *_: (h, 0)
    mat = pl.BlockSpec((half, cols), row_half)
    new_mat = pl.BlockSpec((half, cols), whole)
    vec = pl.BlockSpec((1, half), lambda i, *_: (0, h))
    inputs = [own, near, far, got, w, m, v, g, gm, gv, g_col]
    specs = [mat, new_mat, mat, new_mat, mat, mat, mat, vec, vec, vec]
    specs += [pl.BlockSpec((half, g_col.shape[1]), row_half)]
    n_in = 1 + len(inputs)
    return pl.pallas_call(
        adam_kernel,
        grid_spec=pltpu.PrefetchScalarGridSpec(
            num_scalar_prefetch=1,
            grid=(1,),
            in_specs=specs + [pl.BlockSpec(memory_space=pl.ANY)] * len(carried),
            out_specs=[new_mat, mat, mat, pl.BlockSpec((1, half), whole), vec, vec]
            + [pl.BlockSpec((half + SEND_PAD, cols), whole)],
            scratch_shapes=[pltpu.VMEM((half, 128), F32)],
        ),
        out_shape=[
            shape((half, cols), F32),
            shape((rows, cols), F32),
            shape((rows, cols), F32),
            shape((1, half), F32),
            shape((1, rows), F32),
            shape((1, rows), F32),
            shape((half + SEND_PAD, cols), BF16),
        ],
        input_output_aliases={n_in + k: o for k, o in zip(range(len(carried)), (1, 2, 4, 5))},
        cost_estimate=cost(20 * half * cols, 30 * half * cols),
    )(fix, *inputs, *carried)


def mean_kernel(w, g, got, *refs):
    w_out, g_out = refs[-2:]
    rows = w.shape[0]
    tile = 64

    def step(r, _):
        sl = pl.ds(pl.multiple_of(r * tile, tile), tile)
        w_out[sl, :] = 0.5 * (w[sl, :] + got[sl, :].astype(F32))
        return 0

    lax.fori_loop(0, rows // tile, step, 0)
    g_out[...] = 0.5 * (g[...] + got[rows:, :rows].astype(F32)[:1, :])


def mean_half(h, w_new, g_new, got, carried):
    half, cols = w_new.shape
    rows = 2 * half
    whole = lambda i: (0, 0)
    return pl.pallas_call(
        mean_kernel,
        grid=(1,),
        in_specs=[pl.BlockSpec(a.shape, whole) for a in (w_new, g_new)]
        + [pl.BlockSpec(memory_space=pltpu.VMEM)]
        + [pl.BlockSpec(memory_space=pl.ANY)] * len(carried),
        out_specs=[
            pl.BlockSpec((half, cols), lambda i: (h, 0)),
            pl.BlockSpec((1, half), lambda i: (0, h)),
        ],
        out_shape=[shape((rows, cols), F32), shape((1, rows), F32)],
        input_output_aliases={3 + k: k for k in range(len(carried))},
        cost_estimate=cost(2 * half * cols, 10 * half * cols),
    )(w_new, g_new, got, *carried)


def placed_kernel(own, more, rstd, place, out):
    row_keys = ((own[...] + more[...].astype(F32)) * rstd[:, :1]).astype(BF16)
    out[...] = jnp.dot(place[...], row_keys, preferred_element_type=F32).astype(BF16)


def placed_keys(own, more, rstd, place):
    return pl.pallas_call(
        placed_kernel,
        grid=(1,),
        in_specs=[pl.BlockSpec(own.shape, lambda i: (0, 0))]
        + [pl.BlockSpec(memory_space=pltpu.VMEM)]
        + [pl.BlockSpec(a.shape, lambda i: (0, 0)) for a in (rstd, place)],
        out_specs=pl.BlockSpec(own.shape, lambda i: (0, 0)),
        out_shape=shape(own.shape, BF16),
        cost_estimate=cost(2 * place.size * own.shape[1], 8 * own.size),
        name="placed",
    )(own, more, rstd, place)


def copy_kernel(a, out):
    out[...] = a[...]


def store_keys(a):
    return pl.pallas_call(
        copy_kernel,
        out_shape=pltpu.HBM(a.shape, a.dtype),
        grid=(2,),
        in_specs=[pl.BlockSpec((a.shape[0] // 2, a.shape[1]), lambda i: (i, 0))],
        out_specs=pl.BlockSpec((a.shape[0] // 2, a.shape[1]), lambda i: (i, 0)),
        cost_estimate=cost(0, 4 * a.size),
        name="store",
    )(a)


def finish(bit, reduced, fix, state, g_col, placed):
    give, keep, two_down, three_up, got = reduced
    groups = lax.axis_size("fsdp")
    rows, key_width = placed.shape

    def send(message):
        pairs = [(i, i ^ 1 << bit) for i in range(lax.axis_size("rep"))]
        return lax.ppermute(message, "rep", pairs)

    last = shift(give, 1, 0, 0)
    keys = lax.all_to_all(
        placed.reshape(groups, rows // groups, key_width),
        "fsdp",
        split_axis=0,
        concat_axis=0,
        tiled=True,
    ).reshape(rows, key_width)
    updated, heard, carried = [], [], ()
    for h, other in ((0, got), (1, last)):
        w_new, m, v, g_new, gm, gv, sent = adam_half(
            h, fix, keep, three_up[h], two_down, other, *state, g_col, carried
        )
        carried = (m, v, gm, gv)
        updated.append((w_new, g_new))
        heard.append(send(sent))
    outs = ()
    for h in range(2):
        outs = mean_half(h, *updated[h], heard[h], outs)
    return store_keys(keys), *outs, *carried


def place_kernel(count, dest_row, dest_col, out, *, slot):
    rows = out.shape[0]
    col = lax.broadcasted_iota(I32, (rows, rows), 1)
    row = lax.broadcasted_iota(I32, (rows, rows), 0)
    same = (dest_col[...] == dest_row[...]) & (row < col)
    within = jnp.sum(same.astype(F32), axis=0, keepdims=True).astype(I32)
    lane = lax.broadcasted_iota(I32, (1, rows), 1)
    target = jnp.where(lane < count[0], dest_row[...] * slot + within, -1)
    out[...] = (row == target).astype(F32).astype(BF16)


def placement(count, destination, slot):
    rows = destination.shape[0]
    return pl.pallas_call(
        functools.partial(place_kernel, slot=slot),
        grid_spec=pltpu.PrefetchScalarGridSpec(
            num_scalar_prefetch=1,
            grid=(1,),
            in_specs=[
                pl.BlockSpec((1, rows), lambda i, s: (0, 0)),
                pl.BlockSpec((rows, 1), lambda i, s: (0, 0)),
            ],
            out_specs=pl.BlockSpec((rows, rows), lambda i, s: (0, 0)),
        ),
        out_shape=shape((rows, rows), BF16),
        cost_estimate=cost(4 * rows * rows, 2 * rows * rows),
        name="place",
    )(count, destination[None, :], destination[:, None])


def body(
    tokens,
    cotangent,
    row_count,
    destination,
    step,
    weight,
    weight_m,
    weight_v,
    gain,
    gain_m,
    gain_v,
):
    groups = lax.axis_size("fsdp")
    rows = tokens.shape[0]
    slot = rows // groups
    me = lax.axis_index("fsdp")
    c, z, x = me & 1, me >> 1 & 3, me >> 3
    far_x, far_z = (jnp.array(v, I32) for v in zip(*PLACES))
    ids = ((x + far_x) & 1) * NZ + ((z + far_z) & 3)
    table = 2 * ids + c

    other = shift(tokens, 0, 0, 1)

    half = weight.shape[1] // 2
    tops = []
    for h in range(2):
        sl = slice(h * half, (h + 1) * half)
        narrow = weight[0, sl].astype(BF16).astype(F32)
        narrow_gain = gain[0, sl].astype(BF16).astype(F32)
        tops.append((narrow * narrow_gain[:, None]).astype(BF16))
    top, bottom = tops
    before_top = shift(top, 0, 1, 0)
    after_bottom = shift(bottom, 0, -1, 0)
    own_top = shift(top, 1, 0, 0)
    before_bottom = shift(bottom, 0, 1, 0)
    after_top = shift(top, 0, -1, 0)
    own_bottom = shift(bottom, 1, 0, 0)

    up_own, rstd = prep(row_count, tokens, cotangent)
    up_other = shift(up_own, 0, 0, 1)

    far_top = shift(before_top, 0, 1, 0)
    far_bottom = shift(after_bottom, 0, -1, 0)
    x_before = [shift(before_top, 1, 0, 0), shift(before_bottom, 1, 0, 0)]
    x_after = [shift(after_top, 1, 0, 0), shift(after_bottom, 1, 0, 0)]
    x_far = [shift(far_top, 1, 0, 0), shift(far_bottom, 1, 0, 0)]

    work = (tokens, other, up_own, up_other)
    first_up, first_down = grad_blocks(table, 0, *work, (), BF16, (1, 1))
    adds = (shift(first_up, 0, 1, 0), shift(first_down, 0, -1, 0))
    second_up, second_down = grad_blocks(table, 2, *work, (), BF16, (1, 1))
    two_up = shift(second_up, 0, 1, 0)
    two_down = shift(second_down, 0, -1, 0)
    keep, give = grad_blocks(table, 4, *work, (), F32, (1, 1))
    three_up, three_down = [], []
    for h in range(2):
        third = grad_blocks(table, 6, *work, adds, BF16, (1, 1), 2, h)
        three_up.append(shift(third[0], 0, 1, 0))
        three_down.append(shift(third[1], 0, -1, 0))
    got = shift(add_half(0, give, two_up, three_down[0]), 1, 0, 0)

    near = (top, bottom, before_top, before_bottom, after_top, after_bottom)
    accs = keys_part(table, 8, tokens, other, near, (), (F32, F32))
    near = (far_top, far_bottom, own_top, own_bottom, *x_before, *x_after)
    accs = keys_part(table, 11, tokens, other, near, accs, (F32, F32))
    part_own, part_other = keys_part(table, 15, tokens, other, x_far, accs, (F32, BF16))
    place = placement(row_count, destination, slot)
    placed = placed_keys(part_own, shift(part_other, 0, 0, 1), rstd, place)
    give = add_half(1, give, two_up, three_down[1])

    t = step[0]
    count = (t + 1).astype(F32)
    fix = jnp.stack(
        [
            1.0 - jnp.power(jnp.float32(BETA_ONE), count),
            1.0 - jnp.power(jnp.float32(BETA_TWO), count),
        ]
    )
    bits = min(3, lax.axis_size("rep").bit_length() - 1)
    g_col = jnp.broadcast_to(gain[0][:, None], (gain.shape[1], 128))
    state = (weight[0], weight_m[0], weight_v[0], gain, gain_m, gain_v)
    keys, weight_out, gain_out, m_new, v_new, gm_new, gv_new = lax.switch(
        t % bits,
        [functools.partial(finish, b) for b in range(bits)],
        (give, keep, two_down, tuple(three_up), got),
        fix,
        state,
        g_col,
        placed,
    )
    return keys, weight_out[None], m_new[None], v_new[None], gain_out, gm_new, gv_new


def solution(mesh):
    both, group = P(("rep", "fsdp"), None), P(("rep", "fsdp"))
    mat, vec = P("rep", "fsdp", None), P("rep", "fsdp")
    return jax.shard_map(
        body,
        mesh=mesh,
        in_specs=(both, both, group, group, P(), mat, mat, mat, vec, vec, vec),
        out_specs=(both, mat, mat, mat, vec, vec, vec),
        check_vma=False,
    )
```

```python
import functools

import jax
import jax.numpy as jnp
from jax import lax
from jax.experimental import pallas as pl
from jax.experimental.pallas import tpu as pltpu
from jax.sharding import PartitionSpec as P


BETA_ONE = 0.9
BETA_TWO = 0.95
LEARN_RATE = 0.00015
WEIGHT_DECAY = 0.1
ADAM_EPS = 1e-08
NORM_EPS = 1e-05


BF16, F32, I32 = jnp.bfloat16, jnp.float32, jnp.int32
NX, NZ, NC = 2, 4, 2
PLACES = (
    *((0, 2), (1, 2), (1, 1), (0, 3), (0, 0), (1, 0), (0, 1), (1, 3)),
    *((0, 0), (0, 3), (0, 1), (0, 2), (1, 0), (1, 3), (1, 1), (1, 2)),
)
SEND_PAD = 16


def shape(dims, dtype):
    return jax.ShapeDtypeStruct(dims, dtype)


def place_id(x, z, c):
    return (x % NX * NZ + z % NZ) * NC + c % NC


def shift(a, dx, dz, dc):
    pairs = [
        (place_id(x, z, c), place_id(x + dx, z + dz, c + dc))
        for x in range(NX)
        for z in range(NZ)
        for c in range(NC)
    ]
    return lax.ppermute(a, "fsdp", pairs)


def cost(flops, moved):
    return pl.CostEstimate(flops=flops, transcendentals=0, bytes_accessed=moved)


def prep_kernel(info, x_ref, cot_ref, up_ref, rstd_ref, acc_ref, *, width):
    j = pl.program_id(0)
    rows, block = x_ref.shape
    tile = 64
    for r in range(0, rows, tile):
        parts = [jnp.zeros((tile, 128), F32)] * 4
        for q in range(0, block, 128):
            v = x_ref[r : r + tile, q : q + 128].astype(F32)
            k = q // 128 % 4
            parts[k] = parts[k] + v * v
        part = (parts[0] + parts[1]) + (parts[2] + parts[3])
        acc_ref[r : r + tile, :] = jnp.where(j == 0, part, acc_ref[r : r + tile, :] + part)

    @pl.when(j == pl.num_programs(0) - 1)
    def _():
        count = info[0]
        for r in range(0, rows, tile):
            total = jnp.sum(acc_ref[r : r + tile, :], axis=1, keepdims=True)
            rstd = lax.rsqrt(total * (1.0 / width) + NORM_EPS)
            rstd_ref[r : r + tile, :] = jnp.broadcast_to(rstd, (tile, 128))
            row = lax.broadcasted_iota(I32, (tile, 1), 0) + r
            scale = jnp.where(row < count, rstd, 0.0)
            up_ref[r : r + tile, :] = (cot_ref[r : r + tile, :].astype(F32) * scale).astype(BF16)


def prep(count, tokens, cotangent):
    rows, width = tokens.shape
    key_width = cotangent.shape[1]
    steps = 8
    whole = lambda j, s: (0, 0)
    return pl.pallas_call(
        functools.partial(prep_kernel, width=width),
        grid_spec=pltpu.PrefetchScalarGridSpec(
            num_scalar_prefetch=1,
            grid=(steps,),
            in_specs=[
                pl.BlockSpec((rows, width // steps), lambda j, s: (0, j)),
                pl.BlockSpec((rows, key_width), whole),
            ],
            out_specs=[pl.BlockSpec((rows, key_width), whole), pl.BlockSpec((rows, 128), whole)],
            scratch_shapes=[pltpu.VMEM((rows, 128), F32)],
        ),
        out_shape=[shape((rows, key_width), BF16), shape((rows, 128), F32)],
        cost_estimate=cost(3 * rows * width, 2 * rows * width),
        name="prep",
    )(count, tokens, cotangent)


def over_rows(a, b):
    return lax.dot_general(a, b, (((0,), (0,)), ((), ())), preferred_element_type=F32)


def grad_kernel(table, xa_ref, xb_ref, ua_ref, ub_ref, *refs, n_add, splits):
    adds, outs = refs[:n_add], refs[n_add:]
    s = pl.program_id(0)
    width = xa_ref.shape[1]
    first = 0
    for k, per in enumerate(splits):

        @pl.when(s == k)
        def _(first=first, per=per, k=k):
            tile = width // per
            for p in range(per):
                cols = slice(p * tile, (p + 1) * tile)
                total = over_rows(xa_ref[:, cols], ua_ref[...]) + over_rows(
                    xb_ref[:, cols], ub_ref[...]
                )
                if n_add:
                    total = total + adds[k][cols, :].astype(F32)
                out = outs[first + p]
                out[...] = total.astype(out.dtype)

        first += per


def grad_blocks(table, at, tokens, other, up_own, up_other, adds, dtypes, splits):
    rows, width = tokens.shape
    block = width // (NX * NZ * NC)
    key_width = up_own.shape[1]
    n = len(splits)
    whole = lambda s, t: (0, 0)
    outs = [shape((block // n, key_width), d) for d, n in zip(dtypes, splits) for _ in range(n)]
    return pl.pallas_call(
        functools.partial(grad_kernel, n_add=len(adds), splits=splits),
        grid_spec=pltpu.PrefetchScalarGridSpec(
            num_scalar_prefetch=1,
            grid=(n,),
            in_specs=[
                pl.BlockSpec((rows, block), lambda s, t: (0, t[at + s])),
                pl.BlockSpec((rows, block), lambda s, t: (0, t[at + s])),
                pl.BlockSpec((rows, key_width), whole),
                pl.BlockSpec((rows, key_width), whole),
            ]
            + [pl.BlockSpec((block, key_width), whole) for _ in adds],
            out_specs=[pl.BlockSpec(o.shape, whole) for o in outs],
        ),
        out_shape=outs,
        cost_estimate=cost(
            4 * n * rows * block * key_width,
            4 * n * rows * block + 4 * rows * key_width + 2 * n * block * key_width,
        ),
    )(table, tokens, other, up_own, up_other, *adds)


def add_kernel(own, near, far, out):
    tile = 64

    def step(r, _):
        sl = pl.ds(pl.multiple_of(r * tile, tile), tile)
        total = own[sl, :] + near[sl, :].astype(F32) + far[sl, :].astype(F32)
        out[sl, :] = total.astype(BF16)
        return 0

    lax.fori_loop(0, own.shape[0] // tile, step, 0)


def add_half(h, own, near, far):
    half, cols = far.shape
    part = pl.BlockSpec((half, cols), lambda i: (h, 0))
    whole = pl.BlockSpec((half, cols), lambda i: (0, 0))
    return pl.pallas_call(
        add_kernel,
        grid=(1,),
        in_specs=[part, part, whole],
        out_specs=whole,
        out_shape=shape((half, cols), BF16),
        cost_estimate=cost(2 * half * cols, 10 * half * cols),
    )(own, near, far)


def keys_kernel(table, *refs, n, n_acc):
    xa, xb, rest = refs[:n], refs[n : 2 * n], refs[2 * n :]
    w, rest = rest[: 2 * n], rest[2 * n :]
    accs, outs = rest[:n_acc], rest[n_acc:]
    for x_refs, k in ((xa, 0), (xb, 1)):
        total = accs[k][...] if n_acc else None
        for i, w_ref in enumerate(w):
            depth = w_ref.shape[0]
            lhs = x_refs[i // 2][:, i % 2 * depth : (i % 2 + 1) * depth]
            term = jnp.dot(lhs, w_ref[...], preferred_element_type=F32)
            total = term if total is None else total + term
        outs[k][...] = total.astype(outs[k].dtype)


def keys_part(table, at, tokens, other, pieces, accs, out_dtypes):
    rows, width = tokens.shape
    block = width // (NX * NZ * NC)
    key_width = pieces[0].shape[1]
    tile = rows // 2
    n = len(pieces) // 2
    view_a = lambda q: pl.BlockSpec((tile, block), lambda r, t: (r, t[at + q]))
    view_b = lambda q: pl.BlockSpec((tile, block), lambda r, t: (r, t[at + q]))
    out_spec = pl.BlockSpec((tile, key_width), lambda r, t: (r, 0))
    return pl.pallas_call(
        functools.partial(keys_kernel, n=n, n_acc=len(accs)),
        grid_spec=pltpu.PrefetchScalarGridSpec(
            num_scalar_prefetch=1,
            grid=(rows // tile,),
            in_specs=[view_a(q) for q in range(n)]
            + [view_b(q) for q in range(n)]
            + [pl.BlockSpec(w.shape, lambda r, t: (0, 0)) for w in pieces]
            + [out_spec for _ in accs],
            out_specs=[out_spec, out_spec],
        ),
        out_shape=[shape((rows, key_width), d) for d in out_dtypes],
        cost_estimate=cost(
            4 * n * rows * block * key_width,
            4 * n * rows * block + 2 * n * block * key_width + 8 * rows * key_width,
        ),
    )(table, *([tokens] * n), *([other] * n), *pieces, *accs)


def adam_step(param, first, second, grad, decay, fix_one, fix_two):
    first_new = BETA_ONE * first + (1.0 - BETA_ONE) * grad
    second_new = BETA_TWO * second + (1.0 - BETA_TWO) * grad * grad
    direction = first_new / fix_one / (jnp.sqrt(second_new / fix_two) + ADAM_EPS)
    return (param - LEARN_RATE * (direction + decay * param), first_new, second_new)


def adam_kernel(fix, own, near, far, got, w, m, v, g_row, gm, gv, g_col, *refs):
    (w_new, m_new, v_new, g_new, gm_new, gv_new, sent, fold_ref) = refs[-8:]
    rows, cols = own.shape
    fix_one, fix_two = fix[0], fix[1]
    tile = 32

    def step(r, _):
        sl = pl.ds(pl.multiple_of(r * tile, tile), tile)
        unit = own[sl, :] + near[sl, :].astype(F32) + far[sl, :].astype(F32)
        unit = unit + got[sl, :].astype(F32)
        weight = w[sl, :]
        narrow = weight.astype(BF16).astype(F32)
        gain = g_col[sl, :1].astype(BF16).astype(F32)
        new, first, second = adam_step(
            weight, m[sl, :], v[sl, :], unit * gain, WEIGHT_DECAY, fix_one, fix_two
        )
        w_new[sl, :], m_new[sl, :], v_new[sl, :] = new, first, second
        sent[sl, :] = new.astype(BF16)
        prod = unit * narrow
        fold = prod[:, :128]
        for q in range(128, cols, 128):
            fold = fold + prod[:, q : q + 128]
        fold_ref[sl, :] = fold
        return 0

    lax.fori_loop(0, rows // tile, step, 0)
    grad = lax.dot_general(
        jnp.ones((8, 128), F32),
        fold_ref[...],
        (((1,), (1,)), ((), ())),
        precision=lax.Precision.HIGHEST,
        preferred_element_type=F32,
    )[:1, :]
    new, first, second = adam_step(g_row[...], gm[...], gv[...], grad, 0.0, fix_one, fix_two)
    g_new[...], gm_new[...], gv_new[...] = new, first, second
    sent[rows:, :] = jnp.zeros((sent.shape[0] - rows, cols), BF16)
    sent[rows:, :rows] = jnp.broadcast_to(new, (sent.shape[0] - rows, rows)).astype(BF16)


def adam_half(h, fix, own, near, far, got, w, m, v, g, gm, gv, g_col, carried):
    rows, cols = w.shape
    half = rows // 2
    whole = lambda i, *_: (0, 0)
    row_half = lambda i, *_: (h, 0)
    mat = pl.BlockSpec((half, cols), row_half)
    new_mat = pl.BlockSpec((half, cols), whole)
    vec = pl.BlockSpec((1, half), lambda i, *_: (0, h))
    inputs = [own, near, far, got, w, m, v, g, gm, gv, g_col]
    specs = [mat, new_mat, mat, new_mat, mat, mat, mat, vec, vec, vec]
    specs += [pl.BlockSpec((half, g_col.shape[1]), row_half)]
    n_in = 1 + len(inputs)
    return pl.pallas_call(
        adam_kernel,
        grid_spec=pltpu.PrefetchScalarGridSpec(
            num_scalar_prefetch=1,
            grid=(1,),
            in_specs=specs + [pl.BlockSpec(memory_space=pl.ANY)] * len(carried),
            out_specs=[new_mat, mat, mat, pl.BlockSpec((1, half), whole), vec, vec]
            + [pl.BlockSpec((half + SEND_PAD, cols), whole)],
            scratch_shapes=[pltpu.VMEM((half, 128), F32)],
        ),
        out_shape=[
            shape((half, cols), F32),
            shape((rows, cols), F32),
            shape((rows, cols), F32),
            shape((1, half), F32),
            shape((1, rows), F32),
            shape((1, rows), F32),
            shape((half + SEND_PAD, cols), BF16),
        ],
        input_output_aliases={n_in + k: o for k, o in zip(range(len(carried)), (1, 2, 4, 5))},
        cost_estimate=cost(20 * half * cols, 30 * half * cols),
    )(fix, *inputs, *carried)


def mean_kernel(w, g, got, *refs):
    w_out, g_out = refs[-2:]
    rows = w.shape[0]
    tile = 64

    def step(r, _):
        sl = pl.ds(pl.multiple_of(r * tile, tile), tile)
        w_out[sl, :] = 0.5 * (w[sl, :] + got[sl, :].astype(F32))
        return 0

    lax.fori_loop(0, rows // tile, step, 0)
    g_out[...] = 0.5 * (g[...] + got[rows:, :rows].astype(F32)[:1, :])


def mean_half(h, w_new, g_new, got, carried):
    half, cols = w_new.shape
    rows = 2 * half
    whole = lambda i: (0, 0)
    return pl.pallas_call(
        mean_kernel,
        grid=(1,),
        in_specs=[pl.BlockSpec(a.shape, whole) for a in (w_new, g_new)]
        + [pl.BlockSpec(memory_space=pltpu.VMEM)]
        + [pl.BlockSpec(memory_space=pl.ANY)] * len(carried),
        out_specs=[
            pl.BlockSpec((half, cols), lambda i: (h, 0)),
            pl.BlockSpec((1, half), lambda i: (0, h)),
        ],
        out_shape=[shape((rows, cols), F32), shape((1, rows), F32)],
        input_output_aliases={3 + k: k for k in range(len(carried))},
        cost_estimate=cost(2 * half * cols, 10 * half * cols),
    )(w_new, g_new, got, *carried)


def placed_kernel(own, more, rstd, place, out):
    row_keys = ((own[...] + more[...].astype(F32)) * rstd[:, :1]).astype(BF16)
    out[...] = jnp.dot(place[...], row_keys, preferred_element_type=F32).astype(BF16)


def placed_keys(own, more, rstd, place):
    return pl.pallas_call(
        placed_kernel,
        grid=(1,),
        in_specs=[pl.BlockSpec(own.shape, lambda i: (0, 0))]
        + [pl.BlockSpec(memory_space=pltpu.VMEM)]
        + [pl.BlockSpec(a.shape, lambda i: (0, 0)) for a in (rstd, place)],
        out_specs=pl.BlockSpec(own.shape, lambda i: (0, 0)),
        out_shape=shape(own.shape, BF16),
        cost_estimate=cost(2 * place.size * own.shape[1], 8 * own.size),
        name="placed",
    )(own, more, rstd, place)


def copy_kernel(a, out):
    out[...] = a[...]


def store_keys(a):
    return pl.pallas_call(
        copy_kernel,
        out_shape=pltpu.HBM(a.shape, a.dtype),
        grid=(2,),
        in_specs=[pl.BlockSpec((a.shape[0] // 2, a.shape[1]), lambda i: (i, 0))],
        out_specs=pl.BlockSpec((a.shape[0] // 2, a.shape[1]), lambda i: (i, 0)),
        cost_estimate=cost(0, 4 * a.size),
        name="store",
    )(a)


def finish(bit, reduced, fix, state, g_col, placed):
    give, keep, two_down, three_up, got = reduced
    groups = lax.axis_size("fsdp")
    rows, key_width = placed.shape

    def send(message):
        pairs = [(i, i ^ 1 << bit) for i in range(lax.axis_size("rep"))]
        return lax.ppermute(message, "rep", pairs)

    last = shift(give, 1, 0, 0)
    keys = lax.all_to_all(
        placed.reshape(groups, rows // groups, key_width),
        "fsdp",
        split_axis=0,
        concat_axis=0,
        tiled=True,
    ).reshape(rows, key_width)
    updated, heard, carried = [], [], ()
    for h, other in ((0, got), (1, last)):
        w_new, m, v, g_new, gm, gv, sent = adam_half(
            h, fix, keep, three_up[h], two_down, other, *state, g_col, carried
        )
        carried = (m, v, gm, gv)
        updated.append((w_new, g_new))
        heard.append(send(sent))
    outs = ()
    for h in range(2):
        outs = mean_half(h, *updated[h], heard[h], outs)
    return store_keys(keys), *outs, *carried


def place_kernel(count, dest_row, dest_col, out, *, slot):
    rows = out.shape[0]
    col = lax.broadcasted_iota(I32, (rows, rows), 1)
    row = lax.broadcasted_iota(I32, (rows, rows), 0)
    same = (dest_col[...] == dest_row[...]) & (row < col)
    within = jnp.sum(same.astype(F32), axis=0, keepdims=True).astype(I32)
    lane = lax.broadcasted_iota(I32, (1, rows), 1)
    target = jnp.where(lane < count[0], dest_row[...] * slot + within, -1)
    out[...] = (row == target).astype(F32).astype(BF16)


def placement(count, destination, slot):
    rows = destination.shape[0]
    return pl.pallas_call(
        functools.partial(place_kernel, slot=slot),
        grid_spec=pltpu.PrefetchScalarGridSpec(
            num_scalar_prefetch=1,
            grid=(1,),
            in_specs=[
                pl.BlockSpec((1, rows), lambda i, s: (0, 0)),
                pl.BlockSpec((rows, 1), lambda i, s: (0, 0)),
            ],
            out_specs=pl.BlockSpec((rows, rows), lambda i, s: (0, 0)),
        ),
        out_shape=shape((rows, rows), BF16),
        cost_estimate=cost(4 * rows * rows, 2 * rows * rows),
        name="place",
    )(count, destination[None, :], destination[:, None])


def body(
    tokens,
    cotangent,
    row_count,
    destination,
    step,
    weight,
    weight_m,
    weight_v,
    gain,
    gain_m,
    gain_v,
):
    groups = lax.axis_size("fsdp")
    rows = tokens.shape[0]
    slot = rows // groups
    me = lax.axis_index("fsdp")
    c, z, x = me & 1, me >> 1 & 3, me >> 3
    far_x, far_z = (jnp.array(v, I32) for v in zip(*PLACES))
    ids = ((x + far_x) & 1) * NZ + ((z + far_z) & 3)
    table = 2 * ids + c

    other = shift(tokens, 0, 0, 1)

    half = weight.shape[1] // 2
    tops = []
    for h in range(2):
        sl = slice(h * half, (h + 1) * half)
        narrow = weight[0, sl].astype(BF16).astype(F32)
        narrow_gain = gain[0, sl].astype(BF16).astype(F32)
        tops.append((narrow * narrow_gain[:, None]).astype(BF16))
    top, bottom = tops
    before_top = shift(top, 0, 1, 0)
    after_bottom = shift(bottom, 0, -1, 0)
    own_top = shift(top, 1, 0, 0)
    before_bottom = shift(bottom, 0, 1, 0)
    after_top = shift(top, 0, -1, 0)
    own_bottom = shift(bottom, 1, 0, 0)

    up_own, rstd = prep(row_count, tokens, cotangent)
    up_other = shift(up_own, 0, 0, 1)

    far_top = shift(before_top, 0, 1, 0)
    far_bottom = shift(after_bottom, 0, -1, 0)
    x_before = [shift(before_top, 1, 0, 0), shift(before_bottom, 1, 0, 0)]
    x_after = [shift(after_top, 1, 0, 0), shift(after_bottom, 1, 0, 0)]
    x_far = [shift(far_top, 1, 0, 0), shift(far_bottom, 1, 0, 0)]

    work = (tokens, other, up_own, up_other)
    first_up, first_down = grad_blocks(table, 0, *work, (), (BF16, BF16), (1, 1))
    adds = (shift(first_up, 0, 1, 0), shift(first_down, 0, -1, 0))
    second_up, second_down, keep, give = grad_blocks(
        table, 2, *work, (), (BF16, BF16, F32, F32), (1, 1, 1, 1)
    )
    two_up = shift(second_up, 0, 1, 0)
    two_down = shift(second_down, 0, -1, 0)
    third = grad_blocks(table, 6, *work, adds, (BF16, BF16), (2, 2))
    three_up = [shift(third[h], 0, 1, 0) for h in range(2)]
    three_down = [shift(third[2 + h], 0, -1, 0) for h in range(2)]
    got = shift(add_half(0, give, two_up, three_down[0]), 1, 0, 0)

    near = (top, bottom, before_top, before_bottom, after_top, after_bottom)
    accs = keys_part(table, 8, tokens, other, near, (), (F32, F32))
    near = (far_top, far_bottom, own_top, own_bottom, *x_before, *x_after)
    accs = keys_part(table, 11, tokens, other, near, accs, (F32, F32))
    part_own, part_other = keys_part(table, 15, tokens, other, x_far, accs, (F32, BF16))
    place = placement(row_count, destination, slot)
    placed = placed_keys(part_own, shift(part_other, 0, 0, 1), rstd, place)
    give = add_half(1, give, two_up, three_down[1])

    t = step[0]
    count = (t + 1).astype(F32)
    fix = jnp.stack(
        [
            1.0 - jnp.power(jnp.float32(BETA_ONE), count),
            1.0 - jnp.power(jnp.float32(BETA_TWO), count),
        ]
    )
    bits = min(3, lax.axis_size("rep").bit_length() - 1)
    g_col = jnp.broadcast_to(gain[0][:, None], (gain.shape[1], 128))
    state = (weight[0], weight_m[0], weight_v[0], gain, gain_m, gain_v)
    keys, weight_out, gain_out, m_new, v_new, gm_new, gv_new = lax.switch(
        t % bits,
        [functools.partial(finish, b) for b in range(bits)],
        (give, keep, two_down, tuple(three_up), got),
        fix,
        state,
        g_col,
        placed,
    )
    return keys, weight_out[None], m_new[None], v_new[None], gain_out, gm_new, gv_new


def solution(mesh):
    both, group = P(("rep", "fsdp"), None), P(("rep", "fsdp"))
    mat, vec = P("rep", "fsdp", None), P("rep", "fsdp")
    return jax.shard_map(
        body,
        mesh=mesh,
        in_specs=(both, both, group, group, P(), mat, mat, mat, vec, vec, vec),
        out_specs=(both, mat, mat, mat, vec, vec, vec),
        check_vma=False,
    )
```

```python
import functools

import jax
import jax.numpy as jnp
from jax import lax
from jax.experimental import pallas as pl
from jax.experimental.pallas import tpu as pltpu
from jax.sharding import PartitionSpec as P


BETA_ONE = 0.9
BETA_TWO = 0.95
LEARN_RATE = 0.00015
WEIGHT_DECAY = 0.1
ADAM_EPS = 1e-08
NORM_EPS = 1e-05


BF16, F32, I32 = jnp.bfloat16, jnp.float32, jnp.int32
NX, NZ, NC = 2, 4, 2
PLACES = (
    *((0, 2), (1, 2), (1, 1), (0, 3), (0, 0), (1, 0), (0, 1), (1, 3)),
    *((0, 0), (0, 3), (0, 1), (0, 2), (1, 0), (1, 3), (1, 1), (1, 2)),
)
SEND_PAD = 16


def shape(dims, dtype):
    return jax.ShapeDtypeStruct(dims, dtype)


def place_id(x, z, c):
    return (x % NX * NZ + z % NZ) * NC + c % NC


def shift(a, dx, dz, dc):
    pairs = [
        (place_id(x, z, c), place_id(x + dx, z + dz, c + dc))
        for x in range(NX)
        for z in range(NZ)
        for c in range(NC)
    ]
    return lax.ppermute(a, "fsdp", pairs)


def cost(flops, moved):
    return pl.CostEstimate(flops=flops, transcendentals=0, bytes_accessed=moved)


def prep_kernel(info, x_ref, cot_ref, up_ref, rstd_ref, acc_ref, *, width):
    j = pl.program_id(0)
    rows, block = x_ref.shape
    tile = 64
    for r in range(0, rows, tile):
        parts = [jnp.zeros((tile, 128), F32)] * 4
        for q in range(0, block, 128):
            v = x_ref[r : r + tile, q : q + 128].astype(F32)
            k = q // 128 % 4
            parts[k] = parts[k] + v * v
        part = (parts[0] + parts[1]) + (parts[2] + parts[3])
        acc_ref[r : r + tile, :] = jnp.where(j == 0, part, acc_ref[r : r + tile, :] + part)

    @pl.when(j == pl.num_programs(0) - 1)
    def _():
        count = info[0]
        for r in range(0, rows, tile):
            total = jnp.sum(acc_ref[r : r + tile, :], axis=1, keepdims=True)
            rstd = lax.rsqrt(total * (1.0 / width) + NORM_EPS)
            rstd_ref[r : r + tile, :] = jnp.broadcast_to(rstd, (tile, 128))
            row = lax.broadcasted_iota(I32, (tile, 1), 0) + r
            scale = jnp.where(row < count, rstd, 0.0)
            up_ref[r : r + tile, :] = (cot_ref[r : r + tile, :].astype(F32) * scale).astype(BF16)


def prep(count, tokens, cotangent):
    rows, width = tokens.shape
    key_width = cotangent.shape[1]
    steps = 8
    whole = lambda j, s: (0, 0)
    return pl.pallas_call(
        functools.partial(prep_kernel, width=width),
        grid_spec=pltpu.PrefetchScalarGridSpec(
            num_scalar_prefetch=1,
            grid=(steps,),
            in_specs=[
                pl.BlockSpec((rows, width // steps), lambda j, s: (0, j)),
                pl.BlockSpec((rows, key_width), whole),
            ],
            out_specs=[pl.BlockSpec((rows, key_width), whole), pl.BlockSpec((rows, 128), whole)],
            scratch_shapes=[pltpu.VMEM((rows, 128), F32)],
        ),
        out_shape=[shape((rows, key_width), BF16), shape((rows, 128), F32)],
        cost_estimate=cost(3 * rows * width, 2 * rows * width),
        name="prep",
    )(count, tokens, cotangent)


def over_rows(a, b):
    return lax.dot_general(a, b, (((0,), (0,)), ((), ())), preferred_element_type=F32)


def grad_kernel(table, xa_ref, xb_ref, ua_ref, ub_ref, *refs, n_add, splits):
    adds, outs = refs[:n_add], refs[n_add:]
    s = pl.program_id(0)
    width = xa_ref.shape[1]
    first = 0
    for k, per in enumerate(splits):

        @pl.when(s == k)
        def _(first=first, per=per, k=k):
            tile = width // per
            for p in range(per):
                cols = slice(p * tile, (p + 1) * tile)
                total = over_rows(xa_ref[:, cols], ua_ref[...]) + over_rows(
                    xb_ref[:, cols], ub_ref[...]
                )
                if n_add:
                    total = total + adds[k][cols, :].astype(F32)
                out = outs[first + p]
                out[...] = total.astype(out.dtype)

        first += per


def grad_blocks(table, at, tokens, other, up_own, up_other, adds, dtypes, splits):
    rows, width = tokens.shape
    block = width // (NX * NZ * NC)
    key_width = up_own.shape[1]
    n = len(splits)
    whole = lambda s, t: (0, 0)
    outs = [shape((block // n, key_width), d) for d, n in zip(dtypes, splits) for _ in range(n)]
    return pl.pallas_call(
        functools.partial(grad_kernel, n_add=len(adds), splits=splits),
        grid_spec=pltpu.PrefetchScalarGridSpec(
            num_scalar_prefetch=1,
            grid=(n,),
            in_specs=[
                pl.BlockSpec((rows, block), lambda s, t: (0, t[at + s])),
                pl.BlockSpec((rows, block), lambda s, t: (0, t[at + s])),
                pl.BlockSpec((rows, key_width), whole),
                pl.BlockSpec((rows, key_width), whole),
            ]
            + [pl.BlockSpec((block, key_width), whole) for _ in adds],
            out_specs=[pl.BlockSpec(o.shape, whole) for o in outs],
        ),
        out_shape=outs,
        cost_estimate=cost(
            4 * n * rows * block * key_width,
            4 * n * rows * block + 4 * rows * key_width + 2 * n * block * key_width,
        ),
    )(table, tokens, other, up_own, up_other, *adds)


def add_kernel(own, near, far, out):
    tile = 64

    def step(r, _):
        sl = pl.ds(pl.multiple_of(r * tile, tile), tile)
        total = own[sl, :] + near[sl, :].astype(F32) + far[sl, :].astype(F32)
        out[sl, :] = total.astype(BF16)
        return 0

    lax.fori_loop(0, own.shape[0] // tile, step, 0)


def add_half(h, own, near, far):
    half, cols = far.shape
    part = pl.BlockSpec((half, cols), lambda i: (h, 0))
    whole = pl.BlockSpec((half, cols), lambda i: (0, 0))
    return pl.pallas_call(
        add_kernel,
        grid=(1,),
        in_specs=[part, whole, whole],
        out_specs=whole,
        out_shape=shape((half, cols), BF16),
        cost_estimate=cost(2 * half * cols, 10 * half * cols),
    )(own, near, far)


def keys_kernel(table, *refs, n, n_acc):
    xa, xb, rest = refs[:n], refs[n : 2 * n], refs[2 * n :]
    w, rest = rest[: 2 * n], rest[2 * n :]
    accs, outs = rest[:n_acc], rest[n_acc:]
    for x_refs, k in ((xa, 0), (xb, 1)):
        total = accs[k][...] if n_acc else None
        for i, w_ref in enumerate(w):
            depth = w_ref.shape[0]
            lhs = x_refs[i // 2][:, i % 2 * depth : (i % 2 + 1) * depth]
            term = jnp.dot(lhs, w_ref[...], preferred_element_type=F32)
            total = term if total is None else total + term
        outs[k][...] = total.astype(outs[k].dtype)


def keys_part(table, at, tokens, other, pieces, accs, out_dtypes):
    rows, width = tokens.shape
    block = width // (NX * NZ * NC)
    key_width = pieces[0].shape[1]
    tile = rows // 2
    n = len(pieces) // 2
    view_a = lambda q: pl.BlockSpec((tile, block), lambda r, t: (r, t[at + q]))
    view_b = lambda q: pl.BlockSpec((tile, block), lambda r, t: (r, t[at + q]))
    out_spec = pl.BlockSpec((tile, key_width), lambda r, t: (r, 0))
    return pl.pallas_call(
        functools.partial(keys_kernel, n=n, n_acc=len(accs)),
        grid_spec=pltpu.PrefetchScalarGridSpec(
            num_scalar_prefetch=1,
            grid=(rows // tile,),
            in_specs=[view_a(q) for q in range(n)]
            + [view_b(q) for q in range(n)]
            + [pl.BlockSpec(w.shape, lambda r, t: (0, 0)) for w in pieces]
            + [out_spec for _ in accs],
            out_specs=[out_spec, out_spec],
        ),
        out_shape=[shape((rows, key_width), d) for d in out_dtypes],
        cost_estimate=cost(
            4 * n * rows * block * key_width,
            4 * n * rows * block + 2 * n * block * key_width + 8 * rows * key_width,
        ),
    )(table, *([tokens] * n), *([other] * n), *pieces, *accs)


def moments(first, second, grad):
    first_new = BETA_ONE * first + (1.0 - BETA_ONE) * grad
    return first_new, BETA_TWO * second + (1.0 - BETA_TWO) * grad * grad


def adam_step(param, first, second, grad, decay, scale_one, scale_two):
    first_new, second_new = moments(first, second, grad)
    direction = first_new * scale_one / (jnp.sqrt(second_new * scale_two) + ADAM_EPS)
    return (param - LEARN_RATE * (direction + decay * param), first_new, second_new)


def adam_kernel(fix, own, near, far, got, w, m, v, g_row, gm, gv, g_col, *refs):
    (w_new, g_new, gm_new, gv_new, sent, fold_ref) = refs[-6:]
    rows, cols = own.shape
    fix_one, fix_two = fix[0], fix[1]
    tile, wide = 16, 512

    def step(r, _):
        sl = pl.ds(pl.multiple_of(r * tile, tile), tile)
        gain = g_col[sl, :1].astype(BF16).astype(F32)
        fold = jnp.zeros((tile, 128), F32)
        for c in range(0, cols, wide):
            at = (sl, slice(c, c + wide))
            unit = own[at] + near[at].astype(F32) + far[at].astype(F32)
            unit = unit + got[at].astype(F32)
            weight = w[at]
            prod = unit * weight.astype(BF16).astype(F32)
            for q in range(0, wide, 128):
                fold = fold + prod[:, q : q + 128]
            grad = unit * gain
            new, _, _ = adam_step(weight, m[at], v[at], grad, WEIGHT_DECAY, fix_one, fix_two)
            w_new[at] = new
            sent[at] = new.astype(BF16)
        fold_ref[sl, :] = fold
        return 0

    lax.fori_loop(0, rows // tile, step, 0, unroll=2)
    grad = lax.dot_general(
        jnp.ones((8, 128), F32),
        fold_ref[...],
        (((1,), (1,)), ((), ())),
        precision=lax.Precision.HIGHEST,
        preferred_element_type=F32,
    )[:1, :]
    new, first, second = adam_step(g_row[...], gm[...], gv[...], grad, 0.0, fix_one, fix_two)
    g_new[...], gm_new[...], gv_new[...] = new, first, second
    sent[rows:, :] = jnp.zeros((sent.shape[0] - rows, cols), BF16)
    sent[rows:, :rows] = jnp.broadcast_to(new, (sent.shape[0] - rows, rows)).astype(BF16)


def adam_half(h, fix, own, near, far, got, w, m, v, g, gm, gv, g_col, carried):
    rows, cols = w.shape
    half = rows // 2
    whole = lambda i, *_: (0, 0)
    row_half = lambda i, *_: (h, 0)
    mat = pl.BlockSpec((half, cols), row_half)
    new_mat = pl.BlockSpec((half, cols), whole)
    vec = pl.BlockSpec((1, half), lambda i, *_: (0, h))
    inputs = [own, near, far, got, w, m, v, g, gm, gv, g_col]
    specs = [mat, new_mat, new_mat, new_mat, mat, mat, mat, vec, vec, vec]
    specs += [pl.BlockSpec((half, g_col.shape[1]), row_half)]
    n_in = 1 + len(inputs)
    return pl.pallas_call(
        adam_kernel,
        grid_spec=pltpu.PrefetchScalarGridSpec(
            num_scalar_prefetch=1,
            grid=(1,),
            in_specs=specs + [pl.BlockSpec(memory_space=pl.ANY)] * len(carried),
            out_specs=[new_mat, pl.BlockSpec((1, half), whole), vec, vec]
            + [pl.BlockSpec((half + SEND_PAD, cols), whole)],
            scratch_shapes=[pltpu.VMEM((half, 128), F32)],
        ),
        out_shape=[
            shape((half, cols), F32),
            shape((1, half), F32),
            shape((1, rows), F32),
            shape((1, rows), F32),
            shape((half + SEND_PAD, cols), BF16),
        ],
        input_output_aliases={n_in + k: o for k, o in zip(range(len(carried)), (2, 3))},
        cost_estimate=cost(20 * half * cols, 30 * half * cols),
    )(fix, *inputs, *carried)


def moments_kernel(own, near, far, got, m, v, g_col, *refs):
    m_new, v_new = refs[-2:]
    rows, cols = own.shape
    tile, wide = 16, 512

    def step(r, _):
        sl = pl.ds(pl.multiple_of(r * tile, tile), tile)
        gain = g_col[sl, :1].astype(BF16).astype(F32)
        for c in range(0, cols, wide):
            at = (sl, slice(c, c + wide))
            unit = own[at] + near[at].astype(F32) + far[at].astype(F32)
            grad = (unit + got[at].astype(F32)) * gain
            m_new[at], v_new[at] = moments(m[at], v[at], grad)
        return 0

    lax.fori_loop(0, rows // tile, step, 0, unroll=2)


def moments_half(h, own, near, far, got, m, v, g_col, carried):
    rows, cols = m.shape
    half = rows // 2
    mat = pl.BlockSpec((half, cols), lambda i: (h, 0))
    new_mat = pl.BlockSpec((half, cols), lambda i: (0, 0))
    inputs = [own, near, far, got, m, v, g_col]
    specs = [mat, new_mat, new_mat, new_mat, mat, mat]
    specs += [pl.BlockSpec((half, g_col.shape[1]), lambda i: (h, 0))]
    return pl.pallas_call(
        moments_kernel,
        grid=(1,),
        in_specs=specs + [pl.BlockSpec(memory_space=pl.ANY)] * len(carried),
        out_specs=[mat, mat],
        out_shape=[shape((rows, cols), F32)] * 2,
        input_output_aliases={len(inputs) + k: k for k in range(len(carried))},
        cost_estimate=cost(10 * half * cols, 26 * half * cols),
    )(*inputs, *carried)


def mean_kernel(w, g, got, *refs):
    w_out, g_out = refs[-2:]
    rows = w.shape[0]
    tile = 64

    def step(r, _):
        sl = pl.ds(pl.multiple_of(r * tile, tile), tile)
        w_out[sl, :] = 0.5 * (w[sl, :] + got[sl, :].astype(F32))
        return 0

    lax.fori_loop(0, rows // tile, step, 0)
    g_out[...] = 0.5 * (g[...] + got[rows:, :rows].astype(F32)[:1, :])


def mean_half(h, w_new, g_new, got, carried):
    half, cols = w_new.shape
    rows = 2 * half
    whole = lambda i: (0, 0)
    return pl.pallas_call(
        mean_kernel,
        grid=(1,),
        in_specs=[pl.BlockSpec(a.shape, whole) for a in (w_new, g_new)]
        + [pl.BlockSpec(memory_space=pltpu.VMEM)]
        + [pl.BlockSpec(memory_space=pl.ANY)] * len(carried),
        out_specs=[
            pl.BlockSpec((half, cols), lambda i: (h, 0)),
            pl.BlockSpec((1, half), lambda i: (0, h)),
        ],
        out_shape=[shape((rows, cols), F32), shape((1, rows), F32)],
        input_output_aliases={3 + k: k for k in range(len(carried))},
        cost_estimate=cost(2 * half * cols, 10 * half * cols),
    )(w_new, g_new, got, *carried)


def placed_kernel(own, more, rstd, place, out):
    row_keys = ((own[...] + more[...].astype(F32)) * rstd[:, :1]).astype(BF16)
    out[...] = jnp.dot(place[...], row_keys, preferred_element_type=F32).astype(BF16)


def placed_keys(own, more, rstd, place):
    return pl.pallas_call(
        placed_kernel,
        grid=(1,),
        in_specs=[pl.BlockSpec(own.shape, lambda i: (0, 0))]
        + [pl.BlockSpec(memory_space=pltpu.VMEM)]
        + [pl.BlockSpec(a.shape, lambda i: (0, 0)) for a in (rstd, place)],
        out_specs=pl.BlockSpec(own.shape, lambda i: (0, 0)),
        out_shape=shape(own.shape, BF16),
        cost_estimate=cost(2 * place.size * own.shape[1], 8 * own.size),
        name="placed",
    )(own, more, rstd, place)


def copy_kernel(a, out):
    out[...] = a[...]


def store_keys(a):
    return pl.pallas_call(
        copy_kernel,
        out_shape=pltpu.HBM(a.shape, a.dtype),
        grid=(2,),
        in_specs=[pl.BlockSpec((a.shape[0] // 2, a.shape[1]), lambda i: (i, 0))],
        out_specs=pl.BlockSpec((a.shape[0] // 2, a.shape[1]), lambda i: (i, 0)),
        cost_estimate=cost(0, 4 * a.size),
        name="store",
    )(a)


def finish(bit, reduced, fix, state, g_col, key_parts):
    give, keep, two_down, three_up, got = reduced
    groups = lax.axis_size("fsdp")
    rows, key_width = key_parts[0].shape

    def send(message):
        pairs = [(i, i ^ 1 << bit) for i in range(lax.axis_size("rep"))]
        return lax.ppermute(message, "rep", pairs)

    last = shift(give, 1, 0, 0)
    placed = placed_keys(*key_parts)
    keys = lax.all_to_all(
        placed.reshape(groups, rows // groups, key_width),
        "fsdp",
        split_axis=0,
        concat_axis=0,
        tiled=True,
    ).reshape(rows, key_width)
    updated, heard, gains, held = [], [], (), ()
    others = (got, last)
    for h in range(2):
        sums = (keep, three_up[h], two_down[h], others[h])
        w_new, g_new, gm, gv, sent = adam_half(h, fix, *sums, *state, g_col, gains)
        gains = (gm, gv)
        updated.append((w_new, g_new))
        heard.append(send(sent))
    outs = ()
    for h in range(2):
        sums = (keep, three_up[h], two_down[h], others[h])
        held = moments_half(h, *sums, state[1], state[2], g_col, held)
        outs = mean_half(h, *updated[h], heard[h], outs)
    return store_keys(keys), *outs, *held, *gains


def place_kernel(count, dest_row, dest_col, out, *, slot):
    rows = out.shape[0]
    col = lax.broadcasted_iota(I32, (rows, rows), 1)
    row = lax.broadcasted_iota(I32, (rows, rows), 0)
    same = (dest_col[...] == dest_row[...]) & (row < col)
    within = jnp.sum(same.astype(F32), axis=0, keepdims=True).astype(I32)
    lane = lax.broadcasted_iota(I32, (1, rows), 1)
    target = jnp.where(lane < count[0], dest_row[...] * slot + within, -1)
    out[...] = (row == target).astype(F32).astype(BF16)


def placement(count, destination, slot):
    rows = destination.shape[0]
    return pl.pallas_call(
        functools.partial(place_kernel, slot=slot),
        grid_spec=pltpu.PrefetchScalarGridSpec(
            num_scalar_prefetch=1,
            grid=(1,),
            in_specs=[
                pl.BlockSpec((1, rows), lambda i, s: (0, 0)),
                pl.BlockSpec((rows, 1), lambda i, s: (0, 0)),
            ],
            out_specs=pl.BlockSpec((rows, rows), lambda i, s: (0, 0)),
        ),
        out_shape=shape((rows, rows), BF16),
        cost_estimate=cost(4 * rows * rows, 2 * rows * rows),
        name="place",
    )(count, destination[None, :], destination[:, None])


def body(
    tokens,
    cotangent,
    row_count,
    destination,
    step,
    weight,
    weight_m,
    weight_v,
    gain,
    gain_m,
    gain_v,
):
    groups = lax.axis_size("fsdp")
    rows = tokens.shape[0]
    slot = rows // groups
    me = lax.axis_index("fsdp")
    c, z, x = me & 1, me >> 1 & 3, me >> 3
    far_x, far_z = (jnp.array(v, I32) for v in zip(*PLACES))
    ids = ((x + far_x) & 1) * NZ + ((z + far_z) & 3)
    table = 2 * ids + c

    other = shift(tokens, 0, 0, 1)

    half = weight.shape[1] // 2
    tops = []
    for h in range(2):
        sl = slice(h * half, (h + 1) * half)
        narrow = weight[0, sl].astype(BF16).astype(F32)
        narrow_gain = gain[0, sl].astype(BF16).astype(F32)
        tops.append((narrow * narrow_gain[:, None]).astype(BF16))
    top, bottom = tops
    before_top = shift(top, 0, 1, 0)
    after_bottom = shift(bottom, 0, -1, 0)
    own_top = shift(top, 1, 0, 0)
    before_bottom = shift(bottom, 0, 1, 0)
    after_top = shift(top, 0, -1, 0)
    own_bottom = shift(bottom, 1, 0, 0)

    up_own, rstd = prep(row_count, tokens, cotangent)
    up_other = shift(up_own, 0, 0, 1)

    far_top = shift(before_top, 0, 1, 0)
    far_bottom = shift(after_bottom, 0, -1, 0)
    x_before = [shift(before_top, 1, 0, 0), shift(before_bottom, 1, 0, 0)]
    x_after = [shift(after_top, 1, 0, 0), shift(after_bottom, 1, 0, 0)]
    x_far = [shift(far_top, 1, 0, 0), shift(far_bottom, 1, 0, 0)]

    work = (tokens, other, up_own, up_other)
    first_up, first_down = grad_blocks(table, 0, *work, (), (BF16, BF16), (1, 1))
    adds = (shift(first_up, 0, 1, 0), shift(first_down, 0, -1, 0))
    *second, keep, give = grad_blocks(table, 2, *work, (), (BF16, BF16, F32, F32), (2, 2, 1, 1))
    two_up = [shift(second[h], 0, 1, 0) for h in range(2)]
    two_down = [shift(second[2 + h], 0, -1, 0) for h in range(2)]
    third = grad_blocks(table, 6, *work, adds, (BF16, BF16), (2, 2))
    three_up = [shift(third[h], 0, 1, 0) for h in range(2)]
    three_down = [shift(third[2 + h], 0, -1, 0) for h in range(2)]
    got = shift(add_half(0, give, two_up[0], three_down[0]), 1, 0, 0)

    near = (top, bottom, before_top, before_bottom, after_top, after_bottom)
    accs = keys_part(table, 8, tokens, other, near, (), (F32, F32))
    near = (far_top, far_bottom, own_top, own_bottom, *x_before, *x_after)
    accs = keys_part(table, 11, tokens, other, near, accs, (F32, F32))
    part_own, part_other = keys_part(table, 15, tokens, other, x_far, accs, (F32, BF16))
    place = placement(row_count, destination, slot)
    key_parts = (part_own, shift(part_other, 0, 0, 1), rstd, place)
    give = add_half(1, give, two_up[1], three_down[1])

    t = step[0]
    count = (t + 1).astype(F32)
    fix = jnp.stack(
        [
            1.0 / (1.0 - jnp.power(jnp.float32(BETA_ONE), count)),
            1.0 / (1.0 - jnp.power(jnp.float32(BETA_TWO), count)),
        ]
    )
    bits = min(3, lax.axis_size("rep").bit_length() - 1)
    g_col = jnp.broadcast_to(gain[0][:, None], (gain.shape[1], 128))
    state = (weight[0], weight_m[0], weight_v[0], gain, gain_m, gain_v)
    keys, weight_out, gain_out, m_new, v_new, gm_new, gv_new = lax.switch(
        t % bits,
        [functools.partial(finish, b) for b in range(bits)],
        (give, keep, tuple(two_down), tuple(three_up), got),
        fix,
        state,
        g_col,
        key_parts,
    )
    return keys, weight_out[None], m_new[None], v_new[None], gain_out, gm_new, gv_new


def solution(mesh):
    both, group = P(("rep", "fsdp"), None), P(("rep", "fsdp"))
    mat, vec = P("rep", "fsdp", None), P("rep", "fsdp")
    return jax.shard_map(
        body,
        mesh=mesh,
        in_specs=(both, both, group, group, P(), mat, mat, mat, vec, vec, vec),
        out_specs=(both, mat, mat, mat, vec, vec, vec),
        check_vma=False,
    )
```

```python
import functools

import jax
import jax.numpy as jnp
from jax import lax
from jax.experimental import pallas as pl
from jax.experimental.pallas import tpu as pltpu
from jax.sharding import PartitionSpec as P


BETA_ONE = 0.9
BETA_TWO = 0.95
LEARN_RATE = 0.00015
WEIGHT_DECAY = 0.1
ADAM_EPS = 1e-08
NORM_EPS = 1e-05


BF16, F32, I32 = jnp.bfloat16, jnp.float32, jnp.int32
NX, NZ, NC = 2, 4, 2
PLACES = (
    *((0, 2), (1, 2), (1, 1), (0, 3), (0, 0), (1, 0), (0, 1), (1, 3)),
    *((0, 0), (0, 3), (0, 1), (0, 2), (1, 0), (1, 3), (1, 1), (1, 2)),
)
SEND_PAD = 16


def shape(dims, dtype):
    return jax.ShapeDtypeStruct(dims, dtype)


def place_id(x, z, c):
    return (x % NX * NZ + z % NZ) * NC + c % NC


def shift(a, dx, dz, dc):
    pairs = [
        (place_id(x, z, c), place_id(x + dx, z + dz, c + dc))
        for x in range(NX)
        for z in range(NZ)
        for c in range(NC)
    ]
    return lax.ppermute(a, "fsdp", pairs)


def cost(flops, moved):
    return pl.CostEstimate(flops=flops, transcendentals=0, bytes_accessed=moved)


def prep_kernel(info, x_ref, cot_ref, up_ref, rstd_ref, acc_ref, *, width):
    j = pl.program_id(0)
    rows, block = x_ref.shape
    tile = 64
    for r in range(0, rows, tile):
        parts = [jnp.zeros((tile, 128), F32)] * 4
        for q in range(0, block, 128):
            v = x_ref[r : r + tile, q : q + 128].astype(F32)
            k = q // 128 % 4
            parts[k] = parts[k] + v * v
        part = (parts[0] + parts[1]) + (parts[2] + parts[3])
        acc_ref[r : r + tile, :] = jnp.where(j == 0, part, acc_ref[r : r + tile, :] + part)

    @pl.when(j == pl.num_programs(0) - 1)
    def _():
        count = info[0]
        for r in range(0, rows, tile):
            total = jnp.sum(acc_ref[r : r + tile, :], axis=1, keepdims=True)
            rstd = lax.rsqrt(total * (1.0 / width) + NORM_EPS)
            rstd_ref[r : r + tile, :] = jnp.broadcast_to(rstd, (tile, 128))
            row = lax.broadcasted_iota(I32, (tile, 1), 0) + r
            scale = jnp.where(row < count, rstd, 0.0)
            up_ref[r : r + tile, :] = (cot_ref[r : r + tile, :].astype(F32) * scale).astype(BF16)


def prep(count, tokens, cotangent):
    rows, width = tokens.shape
    key_width = cotangent.shape[1]
    steps = 8
    whole = lambda j, s: (0, 0)
    return pl.pallas_call(
        functools.partial(prep_kernel, width=width),
        grid_spec=pltpu.PrefetchScalarGridSpec(
            num_scalar_prefetch=1,
            grid=(steps,),
            in_specs=[
                pl.BlockSpec((rows, width // steps), lambda j, s: (0, j)),
                pl.BlockSpec((rows, key_width), whole),
            ],
            out_specs=[pl.BlockSpec((rows, key_width), whole), pl.BlockSpec((rows, 128), whole)],
            scratch_shapes=[pltpu.VMEM((rows, 128), F32)],
        ),
        out_shape=[shape((rows, key_width), BF16), shape((rows, 128), F32)],
        cost_estimate=cost(3 * rows * width, 2 * rows * width),
        name="prep",
    )(count, tokens, cotangent)


def over_rows(a, b):
    return lax.dot_general(a, b, (((0,), (0,)), ((), ())), preferred_element_type=F32)


def grad_kernel(table, xa_ref, xb_ref, ua_ref, ub_ref, *refs, n_add, splits):
    adds, outs = refs[:n_add], refs[n_add:]
    s = pl.program_id(0)
    width = xa_ref.shape[1]
    first = 0
    for k, per in enumerate(splits):

        @pl.when(s == k)
        def _(first=first, per=per, k=k):
            tile = width // per
            for p in range(per):
                cols = slice(p * tile, (p + 1) * tile)
                total = over_rows(xa_ref[:, cols], ua_ref[...]) + over_rows(
                    xb_ref[:, cols], ub_ref[...]
                )
                if n_add:
                    total = total + adds[k][cols, :].astype(F32)
                out = outs[first + p]
                out[...] = total.astype(out.dtype)

        first += per


def grad_blocks(table, at, tokens, other, up_own, up_other, adds, dtypes, splits):
    rows, width = tokens.shape
    block = width // (NX * NZ * NC)
    key_width = up_own.shape[1]
    n = len(splits)
    whole = lambda s, t: (0, 0)
    outs = [shape((block // n, key_width), d) for d, n in zip(dtypes, splits) for _ in range(n)]
    return pl.pallas_call(
        functools.partial(grad_kernel, n_add=len(adds), splits=splits),
        grid_spec=pltpu.PrefetchScalarGridSpec(
            num_scalar_prefetch=1,
            grid=(n,),
            in_specs=[
                pl.BlockSpec((rows, block), lambda s, t: (0, t[at + s])),
                pl.BlockSpec((rows, block), lambda s, t: (0, t[at + s])),
                pl.BlockSpec((rows, key_width), whole),
                pl.BlockSpec((rows, key_width), whole),
            ]
            + [pl.BlockSpec((block, key_width), whole) for _ in adds],
            out_specs=[pl.BlockSpec(o.shape, whole) for o in outs],
        ),
        out_shape=outs,
        cost_estimate=cost(
            4 * n * rows * block * key_width,
            4 * n * rows * block + 4 * rows * key_width + 2 * n * block * key_width,
        ),
    )(table, tokens, other, up_own, up_other, *adds)


def add_kernel(own, near, far, out):
    tile = 64

    def step(r, _):
        sl = pl.ds(pl.multiple_of(r * tile, tile), tile)
        total = own[sl, :] + near[sl, :].astype(F32) + far[sl, :].astype(F32)
        out[sl, :] = total.astype(BF16)
        return 0

    lax.fori_loop(0, own.shape[0] // tile, step, 0)


def add_half(h, own, near, far):
    half, cols = far.shape
    part = pl.BlockSpec((half, cols), lambda i: (h, 0))
    whole = pl.BlockSpec((half, cols), lambda i: (0, 0))
    return pl.pallas_call(
        add_kernel,
        grid=(1,),
        in_specs=[part, whole, whole],
        out_specs=whole,
        out_shape=shape((half, cols), BF16),
        cost_estimate=cost(2 * half * cols, 10 * half * cols),
    )(own, near, far)


def keys_kernel(table, *refs, n, n_acc):
    xa, xb, rest = refs[:n], refs[n : 2 * n], refs[2 * n :]
    w, rest = rest[: 2 * n], rest[2 * n :]
    accs, outs = rest[:n_acc], rest[n_acc:]
    for x_refs, k in ((xa, 0), (xb, 1)):
        total = accs[k][...] if n_acc else None
        for i, w_ref in enumerate(w):
            depth = w_ref.shape[0]
            lhs = x_refs[i // 2][:, i % 2 * depth : (i % 2 + 1) * depth]
            term = jnp.dot(lhs, w_ref[...], preferred_element_type=F32)
            total = term if total is None else total + term
        outs[k][...] = total.astype(outs[k].dtype)


def keys_part(table, at, tokens, other, pieces, accs, out_dtypes):
    rows, width = tokens.shape
    block = width // (NX * NZ * NC)
    key_width = pieces[0].shape[1]
    tile = rows // 2
    n = len(pieces) // 2
    view_a = lambda q: pl.BlockSpec((tile, block), lambda r, t: (r, t[at + q]))
    view_b = lambda q: pl.BlockSpec((tile, block), lambda r, t: (r, t[at + q]))
    out_spec = pl.BlockSpec((tile, key_width), lambda r, t: (r, 0))
    return pl.pallas_call(
        functools.partial(keys_kernel, n=n, n_acc=len(accs)),
        grid_spec=pltpu.PrefetchScalarGridSpec(
            num_scalar_prefetch=1,
            grid=(rows // tile,),
            in_specs=[view_a(q) for q in range(n)]
            + [view_b(q) for q in range(n)]
            + [pl.BlockSpec(w.shape, lambda r, t: (0, 0)) for w in pieces]
            + [out_spec for _ in accs],
            out_specs=[out_spec, out_spec],
        ),
        out_shape=[shape((rows, key_width), d) for d in out_dtypes],
        cost_estimate=cost(
            4 * n * rows * block * key_width,
            4 * n * rows * block + 2 * n * block * key_width + 8 * rows * key_width,
        ),
    )(table, *([tokens] * n), *([other] * n), *pieces, *accs)


def moments(first, second, grad):
    first_new = BETA_ONE * first + (1.0 - BETA_ONE) * grad
    return first_new, BETA_TWO * second + (1.0 - BETA_TWO) * grad * grad


def adam_step(param, first, second, grad, decay, scale_one, scale_two):
    first_new, second_new = moments(first, second, grad)
    direction = first_new * scale_one / (jnp.sqrt(second_new * scale_two) + ADAM_EPS)
    return (param - LEARN_RATE * (direction + decay * param), first_new, second_new)


def adam_kernel(fix, own, near, far, got, w, m, v, g_row, gm, gv, g_col, *refs):
    (w_new, g_new, gm_new, gv_new, sent, fold_ref) = refs[-6:]
    rows, cols = own.shape
    fix_one, fix_two = fix[0], fix[1]
    tile, wide = 16, 512

    def step(r, _):
        sl = pl.ds(pl.multiple_of(r * tile, tile), tile)
        gain = g_col[sl, :1].astype(BF16).astype(F32)
        fold = jnp.zeros((tile, 128), F32)
        for c in range(0, cols, wide):
            at = (sl, slice(c, c + wide))
            unit = own[at] + near[at].astype(F32) + far[at].astype(F32)
            unit = unit + got[at].astype(F32)
            weight = w[at]
            prod = unit * weight.astype(BF16).astype(F32)
            for q in range(0, wide, 128):
                fold = fold + prod[:, q : q + 128]
            grad = unit * gain
            new, _, _ = adam_step(weight, m[at], v[at], grad, WEIGHT_DECAY, fix_one, fix_two)
            w_new[at] = new
            sent[at] = new.astype(BF16)
        fold_ref[sl, :] = fold
        return 0

    lax.fori_loop(0, rows // tile, step, 0, unroll=2)
    grad = lax.dot_general(
        jnp.ones((8, 128), F32),
        fold_ref[...],
        (((1,), (1,)), ((), ())),
        precision=lax.Precision.HIGHEST,
        preferred_element_type=F32,
    )[:1, :]
    new, first, second = adam_step(g_row[...], gm[...], gv[...], grad, 0.0, fix_one, fix_two)
    g_new[...], gm_new[...], gv_new[...] = new, first, second
    sent[rows:, :] = jnp.zeros((sent.shape[0] - rows, cols), BF16)
    sent[rows:, :rows] = jnp.broadcast_to(new, (sent.shape[0] - rows, rows)).astype(BF16)


def adam_half(h, fix, own, near, far, got, w, m, v, g, gm, gv, g_col, carried):
    rows, cols = w.shape
    half = rows // 2
    whole = lambda i, *_: (0, 0)
    row_half = lambda i, *_: (h, 0)
    mat = pl.BlockSpec((half, cols), row_half)
    new_mat = pl.BlockSpec((half, cols), whole)
    vec = pl.BlockSpec((1, half), lambda i, *_: (0, h))
    inputs = [own, near, far, got, w, m, v, g, gm, gv, g_col]
    specs = [mat, new_mat, new_mat, new_mat, mat, mat, mat, vec, vec, vec]
    specs += [pl.BlockSpec((half, g_col.shape[1]), row_half)]
    n_in = 1 + len(inputs)
    return pl.pallas_call(
        adam_kernel,
        grid_spec=pltpu.PrefetchScalarGridSpec(
            num_scalar_prefetch=1,
            grid=(1,),
            in_specs=specs + [pl.BlockSpec(memory_space=pl.ANY)] * len(carried),
            out_specs=[new_mat, pl.BlockSpec((1, half), whole), vec, vec]
            + [pl.BlockSpec((half + SEND_PAD, cols), whole)],
            scratch_shapes=[pltpu.VMEM((half, 128), F32)],
        ),
        out_shape=[
            shape((half, cols), F32),
            shape((1, half), F32),
            shape((1, rows), F32),
            shape((1, rows), F32),
            shape((half + SEND_PAD, cols), BF16),
        ],
        input_output_aliases={n_in + k: o for k, o in zip(range(len(carried)), (2, 3))},
        cost_estimate=cost(20 * half * cols, 30 * half * cols),
    )(fix, *inputs, *carried)


def moments_kernel(own, near, far, got, m, v, g_col, *refs):
    m_new, v_new = refs[-2:]
    rows, cols = own.shape
    tile, wide = 16, 512

    def step(r, _):
        sl = pl.ds(pl.multiple_of(r * tile, tile), tile)
        gain = g_col[sl, :1].astype(BF16).astype(F32)
        for c in range(0, cols, wide):
            at = (sl, slice(c, c + wide))
            unit = own[at] + near[at].astype(F32) + far[at].astype(F32)
            grad = (unit + got[at].astype(F32)) * gain
            m_new[at], v_new[at] = moments(m[at], v[at], grad)
        return 0

    lax.fori_loop(0, rows // tile, step, 0, unroll=2)


def moments_half(h, own, near, far, got, m, v, g_col, carried):
    rows, cols = m.shape
    half = rows // 2
    mat = pl.BlockSpec((half, cols), lambda i: (h, 0))
    new_mat = pl.BlockSpec((half, cols), lambda i: (0, 0))
    inputs = [own, near, far, got, m, v, g_col]
    specs = [mat, new_mat, new_mat, new_mat, mat, mat]
    specs += [pl.BlockSpec((half, g_col.shape[1]), lambda i: (h, 0))]
    return pl.pallas_call(
        moments_kernel,
        grid=(1,),
        in_specs=specs + [pl.BlockSpec(memory_space=pl.ANY)] * len(carried),
        out_specs=[mat, mat],
        out_shape=[shape((rows, cols), F32)] * 2,
        input_output_aliases={len(inputs) + k: k for k in range(len(carried))},
        cost_estimate=cost(10 * half * cols, 26 * half * cols),
    )(*inputs, *carried)


def mean_kernel(w, g, got, *refs):
    w_out, g_out = refs[-2:]
    rows = w.shape[0]
    tile = 64

    def step(r, _):
        sl = pl.ds(pl.multiple_of(r * tile, tile), tile)
        w_out[sl, :] = 0.5 * (w[sl, :] + got[sl, :].astype(F32))
        return 0

    lax.fori_loop(0, rows // tile, step, 0)
    g_out[...] = 0.5 * (g[...] + got[rows:, :rows].astype(F32)[:1, :])


def mean_half(h, w_new, g_new, got, carried):
    half, cols = w_new.shape
    rows = 2 * half
    whole = lambda i: (0, 0)
    return pl.pallas_call(
        mean_kernel,
        grid=(1,),
        in_specs=[pl.BlockSpec(a.shape, whole) for a in (w_new, g_new)]
        + [pl.BlockSpec(memory_space=pltpu.VMEM)]
        + [pl.BlockSpec(memory_space=pl.ANY)] * len(carried),
        out_specs=[
            pl.BlockSpec((half, cols), lambda i: (h, 0)),
            pl.BlockSpec((1, half), lambda i: (0, h)),
        ],
        out_shape=[shape((rows, cols), F32), shape((1, rows), F32)],
        input_output_aliases={3 + k: k for k in range(len(carried))},
        cost_estimate=cost(2 * half * cols, 10 * half * cols),
    )(w_new, g_new, got, *carried)


def placed_kernel(own, more, rstd, place, out):
    row_keys = ((own[...] + more[...].astype(F32)) * rstd[:, :1]).astype(BF16)
    out[...] = jnp.dot(place[...], row_keys, preferred_element_type=F32).astype(BF16)


def placed_keys(own, more, rstd, place):
    return pl.pallas_call(
        placed_kernel,
        grid=(1,),
        in_specs=[pl.BlockSpec(own.shape, lambda i: (0, 0))]
        + [pl.BlockSpec(memory_space=pltpu.VMEM)]
        + [pl.BlockSpec(a.shape, lambda i: (0, 0)) for a in (rstd, place)],
        out_specs=pl.BlockSpec(own.shape, lambda i: (0, 0)),
        out_shape=shape(own.shape, BF16),
        cost_estimate=cost(2 * place.size * own.shape[1], 8 * own.size),
        name="placed",
    )(own, more, rstd, place)


def copy_kernel(a, out):
    out[...] = a[...]


def store_keys(a):
    return pl.pallas_call(
        copy_kernel,
        out_shape=pltpu.HBM(a.shape, a.dtype),
        grid=(2,),
        in_specs=[pl.BlockSpec((a.shape[0] // 2, a.shape[1]), lambda i: (i, 0))],
        out_specs=pl.BlockSpec((a.shape[0] // 2, a.shape[1]), lambda i: (i, 0)),
        cost_estimate=cost(0, 4 * a.size),
        name="store",
    )(a)


def finish(bit, reduced, fix, state, g_col, placed):
    give, keep, two_down, three_up, got = reduced
    groups = lax.axis_size("fsdp")
    rows, key_width = placed.shape

    def send(message):
        pairs = [(i, i ^ 1 << bit) for i in range(lax.axis_size("rep"))]
        return lax.ppermute(message, "rep", pairs)

    last = shift(give, 1, 0, 0)
    keys = lax.all_to_all(
        placed.reshape(groups, rows // groups, key_width),
        "fsdp",
        split_axis=0,
        concat_axis=0,
        tiled=True,
    ).reshape(rows, key_width)
    updated, heard, gains, held = [], [], (), ()
    others = (got, last)
    for h in range(2):
        sums = (keep, three_up[h], two_down[h], others[h])
        w_new, g_new, gm, gv, sent = adam_half(h, fix, *sums, *state, g_col, gains)
        gains = (gm, gv)
        updated.append((w_new, g_new))
        heard.append(send(sent))
    outs = ()
    for h in range(2):
        sums = (keep, three_up[h], two_down[h], others[h])
        held = moments_half(h, *sums, state[1], state[2], g_col, held)
        outs = mean_half(h, *updated[h], heard[h], outs)
    return store_keys(keys), *outs, *held, *gains


def place_kernel(count, dest_row, dest_col, out, *, slot):
    rows = out.shape[0]
    col = lax.broadcasted_iota(I32, (rows, rows), 1)
    row = lax.broadcasted_iota(I32, (rows, rows), 0)
    same = (dest_col[...] == dest_row[...]) & (row < col)
    within = jnp.sum(same.astype(F32), axis=0, keepdims=True).astype(I32)
    lane = lax.broadcasted_iota(I32, (1, rows), 1)
    target = jnp.where(lane < count[0], dest_row[...] * slot + within, -1)
    out[...] = (row == target).astype(F32).astype(BF16)


def placement(count, destination, slot):
    rows = destination.shape[0]
    return pl.pallas_call(
        functools.partial(place_kernel, slot=slot),
        grid_spec=pltpu.PrefetchScalarGridSpec(
            num_scalar_prefetch=1,
            grid=(1,),
            in_specs=[
                pl.BlockSpec((1, rows), lambda i, s: (0, 0)),
                pl.BlockSpec((rows, 1), lambda i, s: (0, 0)),
            ],
            out_specs=pl.BlockSpec((rows, rows), lambda i, s: (0, 0)),
        ),
        out_shape=shape((rows, rows), BF16),
        cost_estimate=cost(4 * rows * rows, 2 * rows * rows),
        name="place",
    )(count, destination[None, :], destination[:, None])


def body(
    tokens,
    cotangent,
    row_count,
    destination,
    step,
    weight,
    weight_m,
    weight_v,
    gain,
    gain_m,
    gain_v,
):
    groups = lax.axis_size("fsdp")
    rows = tokens.shape[0]
    slot = rows // groups
    me = lax.axis_index("fsdp")
    c, z, x = me & 1, me >> 1 & 3, me >> 3
    far_x, far_z = (jnp.array(v, I32) for v in zip(*PLACES))
    ids = ((x + far_x) & 1) * NZ + ((z + far_z) & 3)
    table = 2 * ids + c

    other = shift(tokens, 0, 0, 1)

    half = weight.shape[1] // 2
    tops = []
    for h in range(2):
        sl = slice(h * half, (h + 1) * half)
        narrow = weight[0, sl].astype(BF16).astype(F32)
        narrow_gain = gain[0, sl].astype(BF16).astype(F32)
        tops.append((narrow * narrow_gain[:, None]).astype(BF16))
    top, bottom = tops
    before_top = shift(top, 0, 1, 0)
    after_bottom = shift(bottom, 0, -1, 0)
    own_top = shift(top, 1, 0, 0)
    before_bottom = shift(bottom, 0, 1, 0)
    after_top = shift(top, 0, -1, 0)
    own_bottom = shift(bottom, 1, 0, 0)

    up_own, rstd = prep(row_count, tokens, cotangent)
    up_other = shift(up_own, 0, 0, 1)

    far_top = shift(before_top, 0, 1, 0)
    far_bottom = shift(after_bottom, 0, -1, 0)
    x_before = [shift(before_top, 1, 0, 0), shift(before_bottom, 1, 0, 0)]
    x_after = [shift(after_top, 1, 0, 0), shift(after_bottom, 1, 0, 0)]
    x_far = [shift(far_top, 1, 0, 0), shift(far_bottom, 1, 0, 0)]

    work = (tokens, other, up_own, up_other)
    first_up, first_down = grad_blocks(table, 0, *work, (), (BF16, BF16), (1, 1))
    adds = (shift(first_up, 0, 1, 0), shift(first_down, 0, -1, 0))
    *second, keep, give = grad_blocks(table, 2, *work, (), (BF16, BF16, F32, F32), (2, 2, 1, 1))
    two_up = [shift(second[h], 0, 1, 0) for h in range(2)]
    two_down = [shift(second[2 + h], 0, -1, 0) for h in range(2)]
    third = grad_blocks(table, 6, *work, adds, (BF16, BF16), (2, 2))
    three_up = [shift(third[h], 0, 1, 0) for h in range(2)]
    three_down = [shift(third[2 + h], 0, -1, 0) for h in range(2)]
    got = shift(add_half(0, give, two_up[0], three_down[0]), 1, 0, 0)

    near = (top, bottom, before_top, before_bottom, after_top, after_bottom)
    accs = keys_part(table, 8, tokens, other, near, (), (F32, F32))
    near = (far_top, far_bottom, own_top, own_bottom, *x_before, *x_after)
    accs = keys_part(table, 11, tokens, other, near, accs, (F32, F32))
    part_own, part_other = keys_part(table, 15, tokens, other, x_far, accs, (F32, BF16))
    place = placement(row_count, destination, slot)
    placed = placed_keys(part_own, shift(part_other, 0, 0, 1), rstd, place)
    give = add_half(1, give, two_up[1], three_down[1])

    t = step[0]
    count = (t + 1).astype(F32)
    fix = jnp.stack(
        [
            1.0 / (1.0 - jnp.power(jnp.float32(BETA_ONE), count)),
            1.0 / (1.0 - jnp.power(jnp.float32(BETA_TWO), count)),
        ]
    )
    bits = min(3, lax.axis_size("rep").bit_length() - 1)
    g_col = jnp.broadcast_to(gain[0][:, None], (gain.shape[1], 128))
    state = (weight[0], weight_m[0], weight_v[0], gain, gain_m, gain_v)
    keys, weight_out, gain_out, m_new, v_new, gm_new, gv_new = lax.switch(
        t % bits,
        [functools.partial(finish, b) for b in range(bits)],
        (give, keep, tuple(two_down), tuple(three_up), got),
        fix,
        state,
        g_col,
        placed,
    )
    return keys, weight_out[None], m_new[None], v_new[None], gain_out, gm_new, gv_new


def solution(mesh):
    both, group = P(("rep", "fsdp"), None), P(("rep", "fsdp"))
    mat, vec = P("rep", "fsdp", None), P("rep", "fsdp")
    return jax.shard_map(
        body,
        mesh=mesh,
        in_specs=(both, both, group, group, P(), mat, mat, mat, vec, vec, vec),
        out_specs=(both, mat, mat, mat, vec, vec, vec),
        check_vma=False,
    )
```
